32 devices in a mesh: wave: 4 (over z), tile: 8 (over y, x, core).
Axes of the slice: x: 2, y: 2, z: 4, core: 2. Of those that a mesh axis runs over, the one named last changes fastest.
Arguments:
- spectral: bfloat16 [640, 2, 64, 1281], P('wave', None, 'tile'), may hold values from -0.083496094 to 0.083496094
- legendre: bfloat16 [640, 8, 1281], P('wave'), may hold values from -0.25 to 0.25
- pair_ids: int32 [640], replicated, may hold values from 0 to 639, each once
Outputs:
- spectral_out: bfloat16 [640, 2, 64, 1281], P('wave', None, 'tile')
The draws below stay inside these ranges and needn't reach their ends.
Inputs may be any that keep to these rules, and one draw needn't show every extreme that they name: A permutation: each pair 0 to 639 appears once; slot s of spectral, legendre and spectral_out holds wavenumbers pair_ids[s] and 1279 - pair_ids[s].
All inputs are finite; a program needn't handle non-finite values.
Results may differ from the reference program's by a relative error of at most 0.0072.
Values may be sent and summed in bfloat16 or wider, within the bound.
A program may use at most 64 MiB of HBM per device.

```python
import math
import jax
import jax.numpy as jnp
from jax import lax

MW = 1280
HALF_LATS = 1280
COLS = 64
PAIRS = 640
NROW = 1281
NLAT = 8
NPTS = 5156


def block_scale(own_key, dims, pieces, smallest, largest):
    level, own = 1.0, jax.random.fold_in(own_key, 6)
    for dim, blocks in pieces:
        heights = jnp.exp(jax.random.uniform(jax.random.fold_in(own, dim), (blocks,), jnp.float32, smallest / len(pieces), largest / len(pieces)))
        level = level * jnp.repeat(heights, dims[dim] // blocks).reshape([-1 if axis == dim else 1 for axis in range(len(dims))])
    return level


def gaussian(rng, extent, scale, most, shards=(), held_as=jnp.bfloat16):
    values = scale * jax.random.normal(rng, extent, jnp.float32)
    if shards:
        values = values * block_scale(rng, extent, shards, -0.22, 0.18)
    return jnp.clip(values, -most, most).astype(held_as)


def setup_inputs(seed: int = 0) -> dict:
    seeds = jax.random.split(jax.random.key(seed), 4)
    return {
        "spectral": gaussian(seeds[0], (PAIRS, 2, COLS, NROW), (0.5 / MW ** 0.5), 0.083496094, ((0, 4), (2, 8))),
        "legendre": gaussian(seeds[1], (PAIRS, NLAT, NROW), (MW // 2) ** -0.5, 0.25, ((0, 4),)),
        "pair_ids": jax.random.permutation(seeds[2], PAIRS).astype(jnp.int32),
    }


def build_table(wavenumbers, local_index, length, inside, synthesis):
    phase_step = wavenumbers[:, None] * local_index[None, :] % length[None, :]
    angles = 2.0 * math.pi * phase_step.astype(jnp.float32) / length[None, :].astype(jnp.float32)
    keep_mask = (2 * wavenumbers[:, None] < length[None, :]) & inside[None, :]
    if synthesis:
        factor = jnp.where(wavenumbers == 0, 1.0, 2.0).astype(jnp.float32)[:, None]
    else:
        factor = jnp.ones((wavenumbers.shape[0], 1), jnp.float32)
    cosine = jnp.where(keep_mask, factor * jnp.cos(angles), 0.0)
    sine_part = jnp.where(keep_mask, -factor * jnp.sin(angles), 0.0)
    return jnp.concatenate([cosine, sine_part], axis=0).astype(jnp.bfloat16)

def cycle_lengths(pair_number, pair_total):
    polar_cycle = pair_number * (HALF_LATS // 2) // pair_total
    cycle_index = jnp.stack([polar_cycle, HALF_LATS - 1 - polar_cycle]).astype(jnp.int32)
    return (cycle_index, 20 + 4 * cycle_index)

def point_layout(points, cycle_len):
    second = points >= cycle_len[0]
    local_index = points - jnp.where(second, cycle_len[0], 0)
    length = jnp.where(second, cycle_len[1], cycle_len[0])
    inside = points < cycle_len[0] + cycle_len[1]
    return (second, local_index, length, inside)

def cycle_scale(cycle_index, cycle_len, lat_count):
    angles = math.pi * (cycle_index.astype(jnp.float32) + 0.5) / (2.0 * HALF_LATS)
    return 40.0 * jnp.sin(angles) / jnp.sqrt(lat_count * cycle_len.astype(jnp.float32))

def grid_products(grid_values):
    layer_count = grid_values.shape[0] // 4
    nodal_samples = grid_values.astype(jnp.float32).reshape(4, layer_count, grid_values.shape[1])
    zonal_velocity = nodal_samples[0]
    meridional_velocity = nodal_samples[1]
    thermal_state = nodal_samples[2]
    moisture_ratio = nodal_samples[3]
    gravity_surface_altitude = lax.cumsum(thermal_state, axis=0, reverse=True) / math.sqrt(layer_count)
    motion_squared_half = 0.5 * (zonal_velocity * zonal_velocity + meridional_velocity * meridional_velocity) + gravity_surface_altitude
    joined_variables = jnp.stack([motion_squared_half, zonal_velocity * thermal_state, meridional_velocity * thermal_state, zonal_velocity * moisture_ratio])
    return joined_variables.reshape(grid_values.shape).astype(jnp.bfloat16)

def reference(spectral, legendre, pair_ids):
    columns = spectral.shape[2]
    row_total = spectral.shape[3]
    lat_count = legendre.shape[1]
    row_index = jnp.arange(row_total, dtype=jnp.int32)
    upper_half = row_index[None, :] >= (MW - pair_ids)[:, None]

    def forward_slot(slot_args):
        table_slot, spec_slot, upper_slot = slot_args
        halves = jnp.stack([jnp.where(upper_slot, 0, spec_slot), jnp.where(upper_slot, spec_slot, 0)])
        result = jnp.einsum('lr,hxcr->lhxc', table_slot.astype(jnp.float32), halves.astype(jnp.float32), precision=lax.Precision.HIGHEST)
        return result.astype(jnp.bfloat16)
    fourier_in = lax.map(forward_slot, (legendre, spectral, upper_half))
    wavenumbers = jnp.concatenate([pair_ids, MW - 1 - pair_ids]).astype(jnp.int32)
    points = jnp.arange(NPTS, dtype=jnp.int32)

    def pair_pass(pair_number):
        cycle_index, cycle_len = cycle_lengths(pair_number, lat_count // 2)
        second, local_index, length, inside = point_layout(points, cycle_len)
        scales = cycle_scale(cycle_index, cycle_len, lat_count)
        lines = lax.dynamic_slice_in_dim(fourier_in, (2 * pair_number).astype(jnp.int32), 2, 1)
        matrix = jnp.transpose(lines, (1, 4, 3, 2, 0)).reshape(2 * columns, 4 * PAIRS)
        synth_table = build_table(wavenumbers, local_index, length, inside, True)
        result = jnp.dot(matrix, synth_table, preferred_element_type=jnp.float32).reshape(2, columns, NPTS)
        grid_values = jnp.where(second[None, :], result[1], result[0]).astype(jnp.bfloat16)
        product = grid_products(grid_values)
        anal_table = build_table(wavenumbers, local_index, length, inside, False)
        split_rows = jnp.concatenate([jnp.where(second[None, :], 0, product), jnp.where(second[None, :], product, 0)], axis=0)
        summed = lax.dot_general(split_rows, anal_table, (((1,), (1,)), ((), ())), preferred_element_type=jnp.float32)
        summed = summed.reshape(2, columns, 4 * PAIRS) * scales[:, None, None]
        return summed.astype(jnp.bfloat16)
    backs = lax.map(pair_pass, jnp.arange(lat_count // 2, dtype=jnp.int32))
    backs = backs.reshape(lat_count // 2, 2, columns, 2, 2, PAIRS)
    back = jnp.transpose(backs, (5, 0, 1, 4, 3, 2)).reshape(PAIRS, lat_count, 2, 2, columns)

    def direct_slot(slot_args):
        table_slot, back_slot, upper_slot = slot_args
        result = jnp.einsum('lr,lhxc->hxcr', table_slot.astype(jnp.float32), back_slot.astype(jnp.float32), precision=lax.Precision.HIGHEST)
        return jnp.where(upper_slot, result[1], result[0]).astype(jnp.bfloat16)
    return lax.map(direct_slot, (legendre, back, upper_half))
```

```python
import functools
import math

import jax
import jax.numpy as jnp
from jax import lax
from jax.experimental import pallas as pl
from jax.experimental.pallas import tpu as pltpu
from jax.sharding import PartitionSpec as P

MW = 1280
HALF_LATS = 1280
PAIRS = 640
NPTS = 5156
LANES = 128
RADIX = 32

F32 = jnp.float32
BF16 = jnp.bfloat16

HALF = MW // 2
GROUP = HALF // 2
GPAD = -(-GROUP // LANES) * LANES
BLOCKS = GPAD // RADIX
SPAN = 16
AHEAD = 3
MESH = pl.DeviceIdType.MESH
NT = (((1,), (1,)), ((), ()))


def dot(a, b):
    return jnp.dot(a, b, preferred_element_type=F32)


def dot_nt(a, b):
    return lax.dot_general(a, b, NT, preferred_element_type=F32)


def middle_kernel(waves, tiles, cols, lat_count, kpad, *refs):
    (coef, ids, out, fx, gsend, grecv, psend, precv, bsend, trig_t, small_c, small_s, hot,
     s1, r1, s2, r2, s3, r3, s4, r4) = refs
    wave, tile = lax.axis_index("wave"), lax.axis_index("tile")
    quarter = NPTS // 4
    halves = 4 * kpad // tiles
    per_d = tiles // 4
    rows = 2 * cols
    slots = coef.shape[2]

    def exchange(axis, here, count, src, dst, send, recv):
        copies = []
        for off in range(1, count):
            peer = lax.rem(here + off, count)
            copy = pltpu.make_async_remote_copy(
                src_ref=src.at[peer], dst_ref=dst.at[here], send_sem=send.at[off],
                recv_sem=recv.at[off], device_id={axis: peer}, device_id_type=MESH,
            )
            copy.start()
            copies.append(copy)
        dst[here] = src[here]
        return copies

    def finish(axis, here, count, src, dst, send, recv):
        for off in range(1, count):
            origin = lax.rem(here + count - off, count)
            pltpu.make_async_remote_copy(
                src_ref=src.at[origin], dst_ref=dst.at[origin], send_sem=send.at[off],
                recv_sem=recv.at[off], device_id={axis: origin}, device_id_type=MESH,
            ).wait_recv()

    barrier = pltpu.get_barrier_semaphore()
    for axis, here, count in (("wave", wave, waves), ("tile", tile, tiles)):
        for off in range(1, count):
            pl.semaphore_signal(
                barrier, inc=1, device_id={axis: lax.rem(here + off, count)}, device_id_type=MESH
            )

    polar = wave * HALF // (lat_count // 2)
    q0 = 5 + polar
    n0, n1 = 4 * q0, NPTS - 4 * q0

    def line(shape, axis):
        return lax.broadcasted_iota(jnp.int32, shape, axis)

    k = line((1, kpad), 1)
    second = k >= q0
    inside = k < quarter
    point = jnp.where(inside, k - jnp.where(second, q0, 0), 0).astype(F32)
    length = jnp.where(second, n1, n0).astype(F32)

    def trig(m):
        whole = m.astype(F32) * point
        phase = whole - jnp.floor(whole / length) * length
        angle = (2.0 * math.pi) * phase / length
        return jnp.cos(angle), jnp.sin(angle)

    r = line((RADIX, 1), 0)
    m = jnp.where(r < 8, 2 * r, 16 * (r - 8))
    m = jnp.where(r >= 12, (r - 12) // 2 * HALF + (r - 12) % 2, m)
    m = jnp.where(r >= 16, 2 * RADIX * (r - 16), m)
    c, s = trig(m)
    outer = 4 * SPAN
    for g in range(4):
        ca, sa, cb, sb = c[16:], s[16:], c[12 + g : 13 + g], s[12 + g : 13 + g]
        small_c[g * SPAN : (g + 1) * SPAN] = ca * cb - sa * sb
        small_s[g * SPAN : (g + 1) * SPAN] = sa * cb + ca * sb
        ca, sa, cb, sb = c[:8], s[:8], c[8 + g : 9 + g], s[8 + g : 9 + g]
        small_c[outer + 8 * g : outer + 8 * g + 8] = ca * cb - sa * sb
        small_s[outer + 8 * g : outer + 8 * g + 8] = sa * cb + ca * sb

    pl.semaphore_wait(barrier, waves + tiles - 2)
    sends = exchange("wave", wave, waves, coef, fx, s1, r1)

    def block(idx, carry):
        g, a = idx // BLOCKS, idx % BLOCKS
        row_a = g * SPAN + a
        ac, as_ = small_c[pl.ds(row_a, 1), :], small_s[pl.ds(row_a, 1), :]
        bc, bs = small_c[outer:, :], small_s[outer:, :]
        at = ((g % 2) * 4 + g // 2) * GPAD + a * RADIX
        cos_at = pl.ds(pl.multiple_of(at, RADIX), RADIX)
        sin_at = pl.ds(pl.multiple_of(at + 2 * GPAD, RADIX), RADIX)
        trig_t[cos_at, :] = (ac * bc - as_ * bs).astype(BF16)
        trig_t[sin_at, :] = (as_ * bc + ac * bs).astype(BF16)
        return carry

    lax.fori_loop(0, 4 * BLOCKS, block, 0)

    lane = line((2 * GPAD, 1), 0)
    par = jnp.where(lane >= GPAD, 1, 0)
    i = lane - par * GPAD
    low = jnp.where(i < GROUP, 2 * i + par, -1)
    high = jnp.where(i < GROUP, HALF - 1 - par - 2 * i, -1)
    pair = ids[...].reshape(1, ids.shape[0])
    hot[0] = jnp.where(pair == low, 1.0, 0.0).astype(BF16)
    hot[1] = jnp.where(pair == high, 1.0, 0.0).astype(BF16)

    row = line((rows, 1), 0)
    n_row = jnp.where(row >= cols, n1, n0)
    cycle = jnp.where(row >= cols, HALF_LATS - 1 - polar, polar)
    weight = 40.0 * jnp.sin(math.pi * (cycle.astype(F32) + 0.5) / (2.0 * HALF_LATS))
    weight = weight / jnp.sqrt(lat_count * n_row.astype(F32))
    ii = line((1, GPAD), 1)
    up = ii % 2 == 0
    sign = jnp.where(up, 1.0, -1.0)

    def wavenumber(h, p):
        return h * HALF + p + 2 * ii

    def table(p):
        return trig_t[p * 4 * GPAD : (p + 1) * 4 * GPAD, :]

    finish("wave", wave, waves, coef, fx, s1, r1)
    terms = [[[], []], [[], []]]
    for h in range(2):
        here = [fx[w, h * 2 * rows : (h + 1) * 2 * rows, :] for w in range(waves)]
        both = dot_nt(jnp.concatenate(here, axis=1), hot[h])
        for p in range(2):
            m = wavenumber(h, p)
            factor = jnp.where(2 * m < n_row, jnp.where(m == 0, 1.0, 2.0), 0.0)
            part = both[:, p * GPAD : (p + 1) * GPAD]
            re, im = part[:rows] * factor, part[rows:] * factor
            cos_side, sin_side = ((re, re), (-im, -im)) if p == 0 else ((re, im), (-im, re))
            for x, (a, b) in enumerate((cos_side, sin_side)):
                terms[p][x].append(jnp.concatenate([a, b * sign]).astype(BF16))
    even = dot(jnp.concatenate(terms[0][0] + terms[0][1], axis=1), table(0))
    odd = dot(jnp.concatenate(terms[1][0] + terms[1][1], axis=1), table(1))

    def lat_of(x, v):
        return jnp.where(
            second, x[v * rows + cols : (v + 1) * rows], x[v * rows : v * rows + cols]
        )

    e0, e1, o0, o1 = lat_of(even, 0), lat_of(even, 1), lat_of(odd, 0), lat_of(odd, 1)
    for d, x in enumerate((e0 + o0, e1 - o1, e0 - o0, e1 + o1)):
        x = x.astype(BF16)
        for t in range(per_d):
            gsend[d * per_d + t] = x[:, t * halves : (t + 1) * halves]
    sends += exchange("tile", tile, tiles, gsend, grecv, s2, r2)
    finish("tile", tile, tiles, gsend, grecv, s2, r2)

    layers = cols * tiles // 4
    per_f = tiles // 4

    def field(f):
        return jnp.concatenate([grecv[f * per_f + t] for t in range(per_f)])

    u, w_, q = field(0).astype(F32), field(1).astype(F32), field(3).astype(F32)
    t16 = field(2)
    tri = jnp.where(line((layers, layers), 1) >= line((layers, layers), 0), 1.0, 0.0)
    geo = dot(tri.astype(BF16), t16) / math.sqrt(layers)
    temp = t16.astype(F32)
    for f, x in enumerate((0.5 * (u * u + w_ * w_) + geo, u * temp, w_ * temp, u * q)):
        x = x.astype(BF16)
        for t in range(per_f):
            psend[f * per_f + t] = x[t * cols : (t + 1) * cols]
    sends += exchange("tile", tile, tiles, psend, precv, s3, r3)
    finish("tile", tile, tiles, psend, precv, s3, r3)

    def quadrant(d):
        x = jnp.concatenate([precv[d * per_d + t].astype(F32) for t in range(per_d)], axis=1)
        return jnp.where(inside, x, 0.0)

    x0, x1, x2, x3 = [quadrant(d) for d in range(4)]

    def by_lat(*variants):
        return jnp.concatenate(
            [jnp.where(keep, v, 0.0) for v in variants for keep in (k < q0, second)]
        ).astype(BF16)

    even_in = by_lat((x0 + x2) + (x1 + x3), (x0 + x2) - (x1 + x3))
    odd_in = by_lat(x0 - x2, x1 - x3)
    even_out, odd_out = dot_nt(even_in, table(0)), dot_nt(odd_in, table(1))
    for h in range(2):
        at_c, at_s = slice(h * GPAD, (h + 1) * GPAD), slice((2 + h) * GPAD, (3 + h) * GPAD)
        ec, es, oc, os_ = even_out[:, at_c], even_out[:, at_s], odd_out[:, at_c], odd_out[:, at_s]
        keep_e = jnp.where(2 * wavenumber(h, 0) < n_row, weight, 0.0)
        keep_o = jnp.where(2 * wavenumber(h, 1) < n_row, weight, 0.0)
        e_re = jnp.where(up, ec[:rows], ec[rows:]) * keep_e
        e_im = -jnp.where(up, es[:rows], es[rows:]) * keep_e
        o_re = (oc[:rows] - sign * os_[rows:]) * keep_o
        o_im = (-os_[:rows] - sign * oc[rows:]) * keep_o
        e_both = jnp.concatenate([e_re, e_im]).astype(BF16)
        o_both = jnp.concatenate([o_re, o_im]).astype(BF16)
        res = (dot(e_both, hot[h, :GPAD]) + dot(o_both, hot[h, GPAD:])).astype(BF16)
        for w in range(waves):
            bsend[w, h * 2 * rows : (h + 1) * 2 * rows, :] = res[:, w * slots : (w + 1) * slots]
    sends += exchange("wave", wave, waves, bsend, out, s4, r4)
    finish("wave", wave, waves, bsend, out, s4, r4)
    for copy in sends:
        copy.wait_send()


def middle(coef, ids, waves, tiles, cols, lat_count):
    slots = coef.shape[2]
    step = max(tiles // 4, 1) * LANES
    kpad = -(-(NPTS // 4) // step) * step
    chunk = (tiles, cols, 4 * kpad // tiles)
    dma = pltpu.SemaphoreType.DMA
    vmem = pl.BlockSpec(memory_space=pltpu.VMEM)
    return pl.pallas_call(
        functools.partial(middle_kernel, waves, tiles, cols, lat_count, kpad),
        out_shape=jax.ShapeDtypeStruct(coef.shape, BF16),
        in_specs=[vmem, vmem],
        out_specs=vmem,
        scratch_shapes=[
            pltpu.VMEM(coef.shape, BF16),
            pltpu.VMEM(chunk, BF16), pltpu.VMEM(chunk, BF16),
            pltpu.VMEM(chunk, BF16), pltpu.VMEM(chunk, BF16),
            pltpu.VMEM(coef.shape, BF16),
            pltpu.VMEM((8 * GPAD, kpad), BF16),
            pltpu.VMEM((4 * SPAN + RADIX, kpad), F32),
            pltpu.VMEM((4 * SPAN + RADIX, kpad), F32),
            pltpu.VMEM((2, 2 * GPAD, waves * slots), BF16),
            dma((waves,)), dma((waves,)), dma((tiles,)), dma((tiles,)),
            dma((tiles,)), dma((tiles,)), dma((waves,)), dma((waves,)),
        ],
        compiler_params=pltpu.CompilerParams(
            collective_id=0, has_side_effects=True, vmem_limit_bytes=40 * 2**20
        ),
        name="middle",
    )(coef, ids)


def halves_of(ids, block, base):
    lane = lax.broadcasted_iota(jnp.int32, block.shape[1:], 1)
    parts = []
    for b in range(block.shape[0]):
        rows = block[b].astype(F32)
        low = lane < MW - ids[base + b]
        both = [jnp.where(low, rows, 0.0), jnp.where(low, 0.0, rows)]
        parts.append(jnp.concatenate(both).astype(BF16))
    return jnp.concatenate(parts)


def same_slot(shape, rows, columns):
    row = lax.broadcasted_iota(jnp.int32, shape, 0) // rows
    return row == lax.broadcasted_iota(jnp.int32, shape, 1) // columns


def fold(rows, columns):
    row = lax.broadcasted_iota(jnp.int32, (rows, columns), 0) % columns
    same = row == lax.broadcasted_iota(jnp.int32, (rows, columns), 1)
    return jnp.where(same, 1.0, 0.0).astype(BF16)


def forward_kernel(take, ids, spectral, legendre, out, spec_v, leg_v, spec_sem, leg_sem):
    slots, lats, row_total = legendre.shape
    fields = spectral.shape[1] * spectral.shape[2]
    base = lax.axis_index("wave") * slots
    copies = []
    for g in range(slots // take):
        at = pl.ds(g * take, take)
        pair = [
            pltpu.make_async_copy(legendre.at[at], leg_v.at[at], leg_sem.at[g]),
            pltpu.make_async_copy(spectral.at[at], spec_v.at[at], spec_sem.at[g]),
        ]
        copies.append(pair)
    for pair in copies[:AHEAD]:
        for copy in pair:
            copy.start()
    shape = (take * 2 * lats, take * fields)
    same = same_slot(shape, 2 * lats, fields)
    folded = fold(take * fields, fields)
    for g, pair in enumerate(copies):
        for copy in pair:
            copy.wait()
        for copy in copies[g + AHEAD] if g + AHEAD < len(copies) else ():
            copy.start()
        here = slice(g * take, (g + 1) * take)
        left = halves_of(ids, leg_v[here], base + g * take)
        right = spec_v[here].astype(F32).reshape(take * fields, row_total).astype(BF16)
        full = jnp.where(same, dot_nt(left, right), 0.0).astype(BF16)
        full = dot(full, folded).astype(BF16)
        out[here] = full.reshape((take,) + out.shape[1:])


def inverse_kernel(take, ids, back, legendre, out, leg_v, out_v, leg_sem, out_sem):
    slots, lats, row_total = legendre.shape
    fields = out.shape[1] * out.shape[2]
    base = lax.axis_index("wave") * slots
    copies = []
    for g in range(slots // take):
        at = pl.ds(g * take, take)
        copies.append(pltpu.make_async_copy(legendre.at[at], leg_v.at[at], leg_sem.at[g]))
        copies[-1].start()
    shape = (take * fields, take * 2 * lats)
    same = same_slot(shape, fields, 2 * lats)
    folded = fold(take * 2 * lats, 2 * lats)
    results = []
    for g, copy in enumerate(copies):
        at = pl.ds(g * take, take)
        here = slice(g * take, (g + 1) * take)
        narrow = back[here].reshape(take * fields, 2 * lats)
        wide = jnp.where(same, dot_nt(narrow, folded), 0.0).astype(BF16)
        copy.wait()
        right = halves_of(ids, leg_v[here], base + g * take)
        out_v[here] = dot(wide, right).reshape((take,) + out.shape[1:]).astype(BF16)
        results.append(pltpu.make_async_copy(out_v.at[at], out.at[at], out_sem.at[g]))
        results[-1].start()
    for copy in results:
        copy.wait()


def local(spectral, legendre, pair_ids):
    slots, _, cols, row_total = spectral.shape
    lat_count = legendre.shape[1]
    waves, tiles = lax.axis_size("wave"), lax.axis_size("tile")
    take = max(b for b in range(1, 17) if slots % b == 0)
    groups = slots // take
    smem = pl.BlockSpec(memory_space=pltpu.SMEM)
    vmem = pl.BlockSpec(memory_space=pltpu.VMEM)
    hbm = pl.BlockSpec(memory_space=pl.ANY)
    dma = pltpu.SemaphoreType.DMA((groups,))
    params = pltpu.CompilerParams(vmem_limit_bytes=60 * 2**20)
    coef = pl.pallas_call(
        functools.partial(forward_kernel, take),
        out_shape=jax.ShapeDtypeStruct((slots, 2 * lat_count, 2 * cols), BF16),
        in_specs=[smem, hbm, hbm],
        out_specs=vmem,
        scratch_shapes=[
            pltpu.VMEM(spectral.shape, BF16), pltpu.VMEM(legendre.shape, BF16), dma, dma,
        ],
        compiler_params=params,
        name="forward",
    )(pair_ids, spectral, legendre)
    coef = coef.reshape(slots, 2, waves, 2, 2, cols).transpose(2, 1, 4, 3, 5, 0)
    coef = coef.reshape(waves, 8 * cols, slots)
    back = middle(coef, pair_ids, waves, tiles, cols, lat_count)
    back = back.reshape(waves, 2, 2, 2, cols, slots).transpose(5, 2, 4, 1, 0, 3)
    back = back.reshape(slots, 2 * cols, 2 * lat_count)
    return pl.pallas_call(
        functools.partial(inverse_kernel, take),
        out_shape=jax.ShapeDtypeStruct(spectral.shape, BF16),
        in_specs=[smem, vmem, hbm],
        out_specs=hbm,
        scratch_shapes=[
            pltpu.VMEM(legendre.shape, BF16), pltpu.VMEM(spectral.shape, BF16), dma, dma,
        ],
        compiler_params=params,
        name="inverse",
    )(pair_ids, back, legendre)


ROWS = 16
UNIT = 8


def iota(shape, axis):
    return lax.broadcasted_iota(jnp.int32, shape, axis)


def split_rows(ids, block, base):
    count, lats, width = block.shape
    lower = iota((2 * lats, width), 0) < lats
    lane = iota((2 * lats, width), 1)
    pattern = jnp.where(lower, lane, -lane).astype(jnp.int16)
    side = iota((2 * lats, 1), 0) < lats
    parts = []
    for b in range(count):
        bound = MW - ids[base + b]
        limit = jnp.where(side, bound, 1 - bound).astype(jnp.int16)
        both = jnp.concatenate([block[b], block[b]])
        parts.append(jnp.where(pattern < limit, both, jnp.zeros((), BF16)))
    return jnp.concatenate(parts)


def lane_parts(shape, axis, waves, cols):
    lane = iota(shape, axis)
    lat = lane // cols % 2 + lane // (8 * cols) * 2
    field = lane % cols + lane // (2 * cols) % 2 * cols
    half = lane // (4 * cols) % 2
    return half * (2 * waves) + lat, field


def wide_forward_kernel(
    take, waves, ids, spectral, legendre, out, spec_v, leg_v, mid, spec_sem, leg_sem
):
    slots, lats, width = legendre.shape
    cols = spectral.shape[2]
    fields = 2 * cols
    base = lax.axis_index("wave") * slots
    copies = []
    for g in range(slots // take):
        at = pl.ds(g * take, take)
        copies.append([
            pltpu.make_async_copy(legendre.at[at], leg_v.at[at], leg_sem.at[g]),
            pltpu.make_async_copy(spectral.at[at], spec_v.at[at], spec_sem.at[g]),
        ])
        for copy in copies[-1]:
            copy.start()
    n = UNIT * ROWS
    lanes = out.shape[1]
    same = same_slot((n, n), ROWS, ROWS)
    row_lane, field_lane = lane_parts((n, lanes), 1, waves, cols)
    spread = jnp.where(iota((n, lanes), 0) % ROWS == field_lane, 1.0, 0.0).astype(BF16)
    keep = iota((n, lanes), 0) % ROWS == row_lane
    gather = jnp.where(iota((ROWS, 2 * n), 0) == iota((ROWS, 2 * n), 1) // ROWS, 1.0, 0.0)
    gather = gather.astype(BF16)

    def finish(g):
        for at in range(g * take, (g + 1) * take, 2 * UNIT):
            parts = []
            for e in (at, at + UNIT):
                part = dot(mid[e * ROWS : e * ROWS + n], spread)
                parts.append(jnp.where(keep, part, 0.0).astype(BF16))
            out[at : at + 2 * UNIT] = dot(gather, jnp.concatenate(parts)).astype(out.dtype)

    for g, pair in enumerate(copies):
        for copy in pair:
            copy.wait()
        if g:
            finish(g - 1)
        for at in range(g * take, (g + 1) * take, UNIT):
            here = slice(at, at + UNIT)
            left = split_rows(ids, leg_v[here], base + at)
            right = spec_v[here].astype(F32).reshape(UNIT * fields, width).astype(BF16)
            full = jnp.where(same, dot_nt(left, right), 0.0).astype(BF16)
            mid[at * ROWS : at * ROWS + n] = full
    finish(len(copies) - 1)


def wide_inverse_kernel(
    take, waves, ids, back, legendre, out, leg_v, out_v, mid, leg_sem, out_sem
):
    slots, lats, width = legendre.shape
    cols = out.shape[2]
    base = lax.axis_index("wave") * slots
    copies = []
    for g in range(slots // take):
        at = pl.ds(g * take, take)
        copies.append(pltpu.make_async_copy(legendre.at[at], leg_v.at[at], leg_sem.at[g]))
        copies[-1].start()
    n = UNIT * ROWS
    lanes = back.shape[1]
    same = same_slot((n, n), ROWS, ROWS)
    row_lane, _ = lane_parts((lanes, n), 0, waves, cols)
    spread = jnp.where(iota((lanes, n), 1) % ROWS == row_lane, 1.0, 0.0).astype(BF16)
    _, field_lane = lane_parts((ROWS, lanes), 1, waves, cols)
    keep = iota((ROWS, lanes), 0) == field_lane

    def prepare(g):
        for at in range(g * take, (g + 1) * take, UNIT):
            rows = []
            for b in range(at, at + UNIT):
                row = jnp.broadcast_to(back[b : b + 1, :], (ROWS, lanes))
                rows.append(jnp.where(keep, row, 0.0).astype(BF16))
            wide = jnp.where(same, dot(jnp.concatenate(rows), spread), 0.0)
            mid[at * ROWS : at * ROWS + n] = wide.astype(BF16)

    prepare(0)
    results = []
    for g, copy in enumerate(copies):
        copy.wait()
        if g + 1 < len(copies):
            prepare(g + 1)
        for at in range(g * take, (g + 1) * take, UNIT):
            here = slice(at, at + UNIT)
            right = split_rows(ids, leg_v[here], base + at)
            res = dot(mid[at * ROWS : at * ROWS + n], right)
            out_v[here] = res.reshape((UNIT,) + out.shape[1:]).astype(BF16)
        at = pl.ds(g * take, take)
        results.append(pltpu.make_async_copy(out_v.at[at], out.at[at], out_sem.at[g]))
        results[-1].start()
    for copy in results:
        copy.wait()


def wide_local(spectral, legendre, pair_ids):
    slots, _, cols, row_total = spectral.shape
    lat_count = legendre.shape[1]
    waves, tiles = lax.axis_size("wave"), lax.axis_size("tile")
    take = 4 * UNIT
    lanes = 4 * lat_count * cols
    smem = pl.BlockSpec(memory_space=pltpu.SMEM)
    vmem = pl.BlockSpec(memory_space=pltpu.VMEM)
    hbm = pl.BlockSpec(memory_space=pl.ANY)
    dma = pltpu.SemaphoreType.DMA((slots // take,))
    params = pltpu.CompilerParams(vmem_limit_bytes=60 * 2**20)
    scratch = [
        pltpu.VMEM(spectral.shape, BF16), pltpu.VMEM((slots * ROWS, UNIT * ROWS), BF16), dma, dma
    ]
    leg_v = pltpu.VMEM(legendre.shape, BF16)
    coef = pl.pallas_call(
        functools.partial(wide_forward_kernel, take, waves),
        out_shape=jax.ShapeDtypeStruct((slots, lanes), BF16),
        in_specs=[smem, hbm, hbm],
        out_specs=vmem,
        scratch_shapes=[scratch[0], leg_v] + scratch[1:],
        compiler_params=params,
        name="forward",
    )(pair_ids, spectral, legendre)
    coef = coef.T.reshape(waves, 8 * cols, slots)
    back = middle(coef, pair_ids, waves, tiles, cols, lat_count)
    back = back.reshape(lanes, slots).T.astype(F32)
    return pl.pallas_call(
        functools.partial(wide_inverse_kernel, take, waves),
        out_shape=jax.ShapeDtypeStruct(spectral.shape, BF16),
        in_specs=[smem, vmem, hbm],
        out_specs=hbm,
        scratch_shapes=[leg_v] + scratch,
        compiler_params=params,
        name="inverse",
    )(pair_ids, back, legendre)


def pick(spectral, legendre, pair_ids):
    slots, _, cols, _ = spectral.shape
    fits = 2 * cols == ROWS and 2 * legendre.shape[1] == ROWS and slots % (4 * UNIT) == 0
    return (wide_local if fits else local)(spectral, legendre, pair_ids)


def solution(mesh):
    placed = (P("wave", None, "tile", None), P("wave", None, None), P())
    return jax.shard_map(
        pick, mesh=mesh, in_specs=placed, out_specs=P("wave", None, "tile", None), check_vma=False
    )
```

```python
import functools
import math

import jax
import jax.numpy as jnp
from jax import lax
from jax.experimental import pallas as pl
from jax.experimental.pallas import tpu as pltpu
from jax.sharding import PartitionSpec as P

MW = 1280
HALF_LATS = 1280
PAIRS = 640
NPTS = 5156
LANES = 128
RADIX = 32

F32 = jnp.float32
BF16 = jnp.bfloat16

HALF = MW // 2
GROUP = HALF // 2
GPAD = -(-GROUP // LANES) * LANES
BLOCKS = GPAD // RADIX
SPAN = 16
AHEAD = 3
MESH = pl.DeviceIdType.MESH
NT = (((1,), (1,)), ((), ()))


def dot(a, b):
    return jnp.dot(a, b, preferred_element_type=F32)


def dot_nt(a, b):
    return lax.dot_general(a, b, NT, preferred_element_type=F32)


def middle_kernel(waves, tiles, cols, lat_count, kpad, *refs):
    (coef, ids, out, fx, gsend, grecv, psend, precv, bsend, trig_t, small_c, small_s, hot,
     s1, r1, s2, r2, s3, r3, s4, r4) = refs
    wave, tile = lax.axis_index("wave"), lax.axis_index("tile")
    quarter = NPTS // 4
    halves = 4 * kpad // tiles
    per_d = tiles // 4
    rows = 2 * cols
    slots = coef.shape[2]

    def exchange(axis, here, count, src, dst, send, recv):
        copies = []
        for off in range(1, count):
            peer = lax.rem(here + off, count)
            copy = pltpu.make_async_remote_copy(
                src_ref=src.at[peer], dst_ref=dst.at[here], send_sem=send.at[off],
                recv_sem=recv.at[off], device_id={axis: peer}, device_id_type=MESH,
            )
            copy.start()
            copies.append(copy)
        dst[here] = src[here]
        return copies

    def finish(axis, here, count, src, dst, send, recv):
        for off in range(1, count):
            origin = lax.rem(here + count - off, count)
            pltpu.make_async_remote_copy(
                src_ref=src.at[origin], dst_ref=dst.at[origin], send_sem=send.at[off],
                recv_sem=recv.at[off], device_id={axis: origin}, device_id_type=MESH,
            ).wait_recv()

    barrier = pltpu.get_barrier_semaphore()
    for axis, here, count in (("wave", wave, waves), ("tile", tile, tiles)):
        for off in range(1, count):
            pl.semaphore_signal(
                barrier, inc=1, device_id={axis: lax.rem(here + off, count)}, device_id_type=MESH
            )

    polar = wave * HALF // (lat_count // 2)
    q0 = 5 + polar
    n0, n1 = 4 * q0, NPTS - 4 * q0

    def line(shape, axis):
        return lax.broadcasted_iota(jnp.int32, shape, axis)

    k = line((1, kpad), 1)
    second = k >= q0
    inside = k < quarter
    point = jnp.where(inside, k - jnp.where(second, q0, 0), 0).astype(F32)
    length = jnp.where(second, n1, n0).astype(F32)

    def trig(m):
        whole = m.astype(F32) * point
        phase = whole - jnp.floor(whole / length) * length
        angle = (2.0 * math.pi) * phase / length
        return jnp.cos(angle), jnp.sin(angle)

    r = line((RADIX, 1), 0)
    m = jnp.where(r < 8, 2 * r, 16 * (r - 8))
    m = jnp.where(r >= 12, (r - 12) // 2 * HALF + (r - 12) % 2, m)
    m = jnp.where(r >= 16, 2 * RADIX * (r - 16), m)
    c, s = trig(m)
    outer = 4 * SPAN
    for g in range(4):
        ca, sa, cb, sb = c[16:], s[16:], c[12 + g : 13 + g], s[12 + g : 13 + g]
        small_c[g * SPAN : (g + 1) * SPAN] = ca * cb - sa * sb
        small_s[g * SPAN : (g + 1) * SPAN] = sa * cb + ca * sb
        ca, sa, cb, sb = c[:8], s[:8], c[8 + g : 9 + g], s[8 + g : 9 + g]
        small_c[outer + 8 * g : outer + 8 * g + 8] = ca * cb - sa * sb
        small_s[outer + 8 * g : outer + 8 * g + 8] = sa * cb + ca * sb

    pl.semaphore_wait(barrier, waves + tiles - 2)
    sends = exchange("wave", wave, waves, coef, fx, s1, r1)

    def block(idx, carry):
        g, a = idx // BLOCKS, idx % BLOCKS
        row_a = g * SPAN + a
        ac, as_ = small_c[pl.ds(row_a, 1), :], small_s[pl.ds(row_a, 1), :]
        bc, bs = small_c[outer:, :], small_s[outer:, :]
        at = ((g % 2) * 4 + g // 2) * GPAD + a * RADIX
        cos_at = pl.ds(pl.multiple_of(at, RADIX), RADIX)
        sin_at = pl.ds(pl.multiple_of(at + 2 * GPAD, RADIX), RADIX)
        trig_t[cos_at, :] = (ac * bc - as_ * bs).astype(BF16)
        trig_t[sin_at, :] = (as_ * bc + ac * bs).astype(BF16)
        return carry

    lax.fori_loop(0, 4 * BLOCKS, block, 0)

    lane = line((2 * GPAD, 1), 0)
    par = jnp.where(lane >= GPAD, 1, 0)
    i = lane - par * GPAD
    low = jnp.where(i < GROUP, 2 * i + par, -1)
    high = jnp.where(i < GROUP, HALF - 1 - par - 2 * i, -1)
    pair = ids[...].reshape(1, ids.shape[0])
    hot[0] = jnp.where(pair == low, 1.0, 0.0).astype(BF16)
    hot[1] = jnp.where(pair == high, 1.0, 0.0).astype(BF16)

    row = line((rows, 1), 0)
    n_row = jnp.where(row >= cols, n1, n0)
    cycle = jnp.where(row >= cols, HALF_LATS - 1 - polar, polar)
    weight = 40.0 * jnp.sin(math.pi * (cycle.astype(F32) + 0.5) / (2.0 * HALF_LATS))
    weight = weight / jnp.sqrt(lat_count * n_row.astype(F32))
    ii = line((1, GPAD), 1)
    up = ii % 2 == 0
    sign = jnp.where(up, 1.0, -1.0)

    def wavenumber(h, p):
        return h * HALF + p + 2 * ii

    def table(p):
        return trig_t[p * 4 * GPAD : (p + 1) * 4 * GPAD, :]

    finish("wave", wave, waves, coef, fx, s1, r1)
    terms = [[[], []], [[], []]]
    for h in range(2):
        here = [fx[w, h * 2 * rows : (h + 1) * 2 * rows, :] for w in range(waves)]
        both = dot_nt(jnp.concatenate(here, axis=1), hot[h])
        for p in range(2):
            m = wavenumber(h, p)
            factor = jnp.where(2 * m < n_row, jnp.where(m == 0, 1.0, 2.0), 0.0)
            part = both[:, p * GPAD : (p + 1) * GPAD]
            re, im = part[:rows] * factor, part[rows:] * factor
            cos_side, sin_side = ((re, re), (-im, -im)) if p == 0 else ((re, im), (-im, re))
            for x, (a, b) in enumerate((cos_side, sin_side)):
                terms[p][x].append(jnp.concatenate([a, b * sign]).astype(BF16))
    even = dot(jnp.concatenate(terms[0][0] + terms[0][1], axis=1), table(0))
    odd = dot(jnp.concatenate(terms[1][0] + terms[1][1], axis=1), table(1))

    def lat_of(x, v):
        return jnp.where(
            second, x[v * rows + cols : (v + 1) * rows], x[v * rows : v * rows + cols]
        )

    e0, e1, o0, o1 = lat_of(even, 0), lat_of(even, 1), lat_of(odd, 0), lat_of(odd, 1)
    for d, x in enumerate((e0 + o0, e1 - o1, e0 - o0, e1 + o1)):
        x = x.astype(BF16)
        for t in range(per_d):
            gsend[d * per_d + t] = x[:, t * halves : (t + 1) * halves]
    sends += exchange("tile", tile, tiles, gsend, grecv, s2, r2)
    finish("tile", tile, tiles, gsend, grecv, s2, r2)

    layers = cols * tiles // 4
    per_f = tiles // 4

    def field(f):
        return jnp.concatenate([grecv[f * per_f + t] for t in range(per_f)])

    u, w_, q = field(0).astype(F32), field(1).astype(F32), field(3).astype(F32)
    t16 = field(2)
    tri = jnp.where(line((layers, layers), 1) >= line((layers, layers), 0), 1.0, 0.0)
    geo = dot(tri.astype(BF16), t16) / math.sqrt(layers)
    temp = t16.astype(F32)
    for f, x in enumerate((0.5 * (u * u + w_ * w_) + geo, u * temp, w_ * temp, u * q)):
        x = x.astype(BF16)
        for t in range(per_f):
            psend[f * per_f + t] = x[t * cols : (t + 1) * cols]
    sends += exchange("tile", tile, tiles, psend, precv, s3, r3)
    finish("tile", tile, tiles, psend, precv, s3, r3)

    def quadrant(d):
        x = jnp.concatenate([precv[d * per_d + t].astype(F32) for t in range(per_d)], axis=1)
        return jnp.where(inside, x, 0.0)

    x0, x1, x2, x3 = [quadrant(d) for d in range(4)]

    def by_lat(*variants):
        return jnp.concatenate(
            [jnp.where(keep, v, 0.0) for v in variants for keep in (k < q0, second)]
        ).astype(BF16)

    even_in = by_lat((x0 + x2) + (x1 + x3), (x0 + x2) - (x1 + x3))
    odd_in = by_lat(x0 - x2, x1 - x3)
    even_out, odd_out = dot_nt(even_in, table(0)), dot_nt(odd_in, table(1))
    for h in range(2):
        at_c, at_s = slice(h * GPAD, (h + 1) * GPAD), slice((2 + h) * GPAD, (3 + h) * GPAD)
        ec, es, oc, os_ = even_out[:, at_c], even_out[:, at_s], odd_out[:, at_c], odd_out[:, at_s]
        keep_e = jnp.where(2 * wavenumber(h, 0) < n_row, weight, 0.0)
        keep_o = jnp.where(2 * wavenumber(h, 1) < n_row, weight, 0.0)
        e_re = jnp.where(up, ec[:rows], ec[rows:]) * keep_e
        e_im = -jnp.where(up, es[:rows], es[rows:]) * keep_e
        o_re = (oc[:rows] - sign * os_[rows:]) * keep_o
        o_im = (-os_[:rows] - sign * oc[rows:]) * keep_o
        e_both = jnp.concatenate([e_re, e_im]).astype(BF16)
        o_both = jnp.concatenate([o_re, o_im]).astype(BF16)
        res = (dot(e_both, hot[h, :GPAD]) + dot(o_both, hot[h, GPAD:])).astype(BF16)
        for w in range(waves):
            bsend[w, h * 2 * rows : (h + 1) * 2 * rows, :] = res[:, w * slots : (w + 1) * slots]
    sends += exchange("wave", wave, waves, bsend, out, s4, r4)
    finish("wave", wave, waves, bsend, out, s4, r4)
    for copy in sends:
        copy.wait_send()


def middle(coef, ids, waves, tiles, cols, lat_count):
    slots = coef.shape[2]
    step = max(tiles // 4, 1) * LANES
    kpad = -(-(NPTS // 4) // step) * step
    chunk = (tiles, cols, 4 * kpad // tiles)
    dma = pltpu.SemaphoreType.DMA
    vmem = pl.BlockSpec(memory_space=pltpu.VMEM)
    return pl.pallas_call(
        functools.partial(middle_kernel, waves, tiles, cols, lat_count, kpad),
        out_shape=jax.ShapeDtypeStruct(coef.shape, BF16),
        in_specs=[vmem, vmem],
        out_specs=vmem,
        scratch_shapes=[
            pltpu.VMEM(coef.shape, BF16),
            pltpu.VMEM(chunk, BF16), pltpu.VMEM(chunk, BF16),
            pltpu.VMEM(chunk, BF16), pltpu.VMEM(chunk, BF16),
            pltpu.VMEM(coef.shape, BF16),
            pltpu.VMEM((8 * GPAD, kpad), BF16),
            pltpu.VMEM((4 * SPAN + RADIX, kpad), F32),
            pltpu.VMEM((4 * SPAN + RADIX, kpad), F32),
            pltpu.VMEM((2, 2 * GPAD, waves * slots), BF16),
            dma((waves,)), dma((waves,)), dma((tiles,)), dma((tiles,)),
            dma((tiles,)), dma((tiles,)), dma((waves,)), dma((waves,)),
        ],
        compiler_params=pltpu.CompilerParams(
            collective_id=0, has_side_effects=True, vmem_limit_bytes=40 * 2**20
        ),
        name="middle",
    )(coef, ids)


def halves_of(ids, block, base):
    lane = lax.broadcasted_iota(jnp.int32, block.shape[1:], 1)
    parts = []
    for b in range(block.shape[0]):
        rows = block[b].astype(F32)
        low = lane < MW - ids[base + b]
        both = [jnp.where(low, rows, 0.0), jnp.where(low, 0.0, rows)]
        parts.append(jnp.concatenate(both).astype(BF16))
    return jnp.concatenate(parts)


def same_slot(shape, rows, columns):
    row = lax.broadcasted_iota(jnp.int32, shape, 0) // rows
    return row == lax.broadcasted_iota(jnp.int32, shape, 1) // columns


def fold(rows, columns):
    row = lax.broadcasted_iota(jnp.int32, (rows, columns), 0) % columns
    same = row == lax.broadcasted_iota(jnp.int32, (rows, columns), 1)
    return jnp.where(same, 1.0, 0.0).astype(BF16)


def forward_kernel(take, ids, spectral, legendre, out, spec_v, leg_v, spec_sem, leg_sem):
    slots, lats, row_total = legendre.shape
    fields = spectral.shape[1] * spectral.shape[2]
    base = lax.axis_index("wave") * slots
    copies = []
    for g in range(slots // take):
        at = pl.ds(g * take, take)
        pair = [
            pltpu.make_async_copy(legendre.at[at], leg_v.at[at], leg_sem.at[g]),
            pltpu.make_async_copy(spectral.at[at], spec_v.at[at], spec_sem.at[g]),
        ]
        copies.append(pair)
    for pair in copies[:AHEAD]:
        for copy in pair:
            copy.start()
    shape = (take * 2 * lats, take * fields)
    same = same_slot(shape, 2 * lats, fields)
    folded = fold(take * fields, fields)
    for g, pair in enumerate(copies):
        for copy in pair:
            copy.wait()
        for copy in copies[g + AHEAD] if g + AHEAD < len(copies) else ():
            copy.start()
        here = slice(g * take, (g + 1) * take)
        left = halves_of(ids, leg_v[here], base + g * take)
        right = spec_v[here].astype(F32).reshape(take * fields, row_total).astype(BF16)
        full = jnp.where(same, dot_nt(left, right), 0.0).astype(BF16)
        full = dot(full, folded).astype(BF16)
        out[here] = full.reshape((take,) + out.shape[1:])


def inverse_kernel(take, ids, back, legendre, out, leg_v, out_v, leg_sem, out_sem):
    slots, lats, row_total = legendre.shape
    fields = out.shape[1] * out.shape[2]
    base = lax.axis_index("wave") * slots
    copies = []
    for g in range(slots // take):
        at = pl.ds(g * take, take)
        copies.append(pltpu.make_async_copy(legendre.at[at], leg_v.at[at], leg_sem.at[g]))
        copies[-1].start()
    shape = (take * fields, take * 2 * lats)
    same = same_slot(shape, fields, 2 * lats)
    folded = fold(take * 2 * lats, 2 * lats)
    results = []
    for g, copy in enumerate(copies):
        at = pl.ds(g * take, take)
        here = slice(g * take, (g + 1) * take)
        narrow = back[here].reshape(take * fields, 2 * lats)
        wide = jnp.where(same, dot_nt(narrow, folded), 0.0).astype(BF16)
        copy.wait()
        right = halves_of(ids, leg_v[here], base + g * take)
        out_v[here] = dot(wide, right).reshape((take,) + out.shape[1:]).astype(BF16)
        results.append(pltpu.make_async_copy(out_v.at[at], out.at[at], out_sem.at[g]))
        results[-1].start()
    for copy in results:
        copy.wait()


def local(spectral, legendre, pair_ids):
    slots, _, cols, row_total = spectral.shape
    lat_count = legendre.shape[1]
    waves, tiles = lax.axis_size("wave"), lax.axis_size("tile")
    take = max(b for b in range(1, 17) if slots % b == 0)
    groups = slots // take
    smem = pl.BlockSpec(memory_space=pltpu.SMEM)
    vmem = pl.BlockSpec(memory_space=pltpu.VMEM)
    hbm = pl.BlockSpec(memory_space=pl.ANY)
    dma = pltpu.SemaphoreType.DMA((groups,))
    params = pltpu.CompilerParams(vmem_limit_bytes=60 * 2**20)
    coef = pl.pallas_call(
        functools.partial(forward_kernel, take),
        out_shape=jax.ShapeDtypeStruct((slots, 2 * lat_count, 2 * cols), BF16),
        in_specs=[smem, hbm, hbm],
        out_specs=vmem,
        scratch_shapes=[
            pltpu.VMEM(spectral.shape, BF16), pltpu.VMEM(legendre.shape, BF16), dma, dma,
        ],
        compiler_params=params,
        name="forward",
    )(pair_ids, spectral, legendre)
    coef = coef.reshape(slots, 2, waves, 2, 2, cols).transpose(2, 1, 4, 3, 5, 0)
    coef = coef.reshape(waves, 8 * cols, slots)
    back = middle(coef, pair_ids, waves, tiles, cols, lat_count)
    back = back.reshape(waves, 2, 2, 2, cols, slots).transpose(5, 2, 4, 1, 0, 3)
    back = back.reshape(slots, 2 * cols, 2 * lat_count)
    return pl.pallas_call(
        functools.partial(inverse_kernel, take),
        out_shape=jax.ShapeDtypeStruct(spectral.shape, BF16),
        in_specs=[smem, vmem, hbm],
        out_specs=hbm,
        scratch_shapes=[
            pltpu.VMEM(legendre.shape, BF16), pltpu.VMEM(spectral.shape, BF16), dma, dma,
        ],
        compiler_params=params,
        name="inverse",
    )(pair_ids, back, legendre)


ROWS = 16
UNIT = 8


def iota(shape, axis):
    return lax.broadcasted_iota(jnp.int32, shape, axis)


def split_rows(ids, block, base):
    count, lats, width = block.shape
    lower = iota((2 * lats, width), 0) < lats
    lane = iota((2 * lats, width), 1)
    pattern = jnp.where(lower, lane, -lane).astype(jnp.int16)
    side = iota((2 * lats, 1), 0) < lats
    parts = []
    for b in range(count):
        bound = MW - ids[base + b]
        limit = jnp.where(side, bound, 1 - bound).astype(jnp.int16)
        both = jnp.concatenate([block[b], block[b]])
        parts.append(jnp.where(pattern < limit, both, jnp.zeros((), BF16)))
    return jnp.concatenate(parts)


def lane_parts(shape, axis, waves, cols):
    lane = iota(shape, axis)
    lat = lane // cols % 2 + lane // (8 * cols) * 2
    field = lane % cols + lane // (2 * cols) % 2 * cols
    half = lane // (4 * cols) % 2
    return half * (2 * waves) + lat, field


def wide_forward_kernel(
    take, waves, ids_in, spectral, legendre, out,
    spec_v, leg_v, mid, spec_sem, leg_sem, ids, ids_sem
):
    slots, lats, width = legendre.shape
    cols = spectral.shape[2]
    fields = 2 * cols
    base = lax.axis_index("wave") * slots
    ids_copy = pltpu.make_async_copy(ids_in, ids, ids_sem)
    ids_copy.start()
    copies = []
    for g in range(slots // take):
        at = pl.ds(g * take, take)
        copies.append([
            pltpu.make_async_copy(legendre.at[at], leg_v.at[at], leg_sem.at[g]),
            pltpu.make_async_copy(spectral.at[at], spec_v.at[at], spec_sem.at[g]),
        ])
        for copy in copies[-1]:
            copy.start()
    n = UNIT * ROWS
    lanes = out.shape[1]
    same = same_slot((n, n), ROWS, ROWS)
    row_lane, field_lane = lane_parts((n, lanes), 1, waves, cols)
    spread = jnp.where(iota((n, lanes), 0) % ROWS == field_lane, 1.0, 0.0).astype(BF16)
    keep = iota((n, lanes), 0) % ROWS == row_lane
    gather = jnp.where(iota((ROWS, 2 * n), 0) == iota((ROWS, 2 * n), 1) // ROWS, 1.0, 0.0)
    gather = gather.astype(BF16)

    def finish(g):
        for at in range(g * take, (g + 1) * take, 2 * UNIT):
            parts = []
            for e in (at, at + UNIT):
                part = dot(mid[e * ROWS : e * ROWS + n], spread)
                parts.append(jnp.where(keep, part, 0.0).astype(BF16))
            out[at : at + 2 * UNIT] = dot(gather, jnp.concatenate(parts)).astype(out.dtype)

    ids_copy.wait()
    for g, pair in enumerate(copies):
        for copy in pair:
            copy.wait()
        if g:
            finish(g - 1)
        for at in range(g * take, (g + 1) * take, UNIT):
            here = slice(at, at + UNIT)
            left = split_rows(ids, leg_v[here], base + at)
            right = spec_v[here].astype(F32).reshape(UNIT * fields, width).astype(BF16)
            full = jnp.where(same, dot_nt(left, right), 0.0).astype(BF16)
            mid[at * ROWS : at * ROWS + n] = full
    finish(len(copies) - 1)


def wide_inverse_kernel(
    take, waves, ids_in, back, legendre, out,
    leg_v, out_v, mid, leg_sem, out_sem, ids, ids_sem
):
    slots, lats, width = legendre.shape
    cols = out.shape[2]
    base = lax.axis_index("wave") * slots
    ids_copy = pltpu.make_async_copy(ids_in, ids, ids_sem)
    ids_copy.start()
    copies = []
    for g in range(slots // take):
        at = pl.ds(g * take, take)
        copies.append(pltpu.make_async_copy(legendre.at[at], leg_v.at[at], leg_sem.at[g]))
        copies[-1].start()
    n = UNIT * ROWS
    lanes = back.shape[1]
    same = same_slot((n, n), ROWS, ROWS)
    row_lane, _ = lane_parts((lanes, n), 0, waves, cols)
    spread = jnp.where(iota((lanes, n), 1) % ROWS == row_lane, 1.0, 0.0).astype(BF16)
    _, field_lane = lane_parts((ROWS, lanes), 1, waves, cols)
    keep = iota((ROWS, lanes), 0) == field_lane

    def prepare(g):
        for at in range(g * take, (g + 1) * take, UNIT):
            rows = []
            for b in range(at, at + UNIT):
                row = jnp.broadcast_to(back[b : b + 1, :], (ROWS, lanes))
                rows.append(jnp.where(keep, row, 0.0).astype(BF16))
            wide = jnp.where(same, dot(jnp.concatenate(rows), spread), 0.0)
            mid[at * ROWS : at * ROWS + n] = wide.astype(BF16)

    prepare(0)
    ids_copy.wait()
    results = []
    for g, copy in enumerate(copies):
        copy.wait()
        if g + 1 < len(copies):
            prepare(g + 1)
        for at in range(g * take, (g + 1) * take, UNIT):
            here = slice(at, at + UNIT)
            right = split_rows(ids, leg_v[here], base + at)
            res = dot(mid[at * ROWS : at * ROWS + n], right)
            out_v[here] = res.reshape((UNIT,) + out.shape[1:]).astype(BF16)
        at = pl.ds(g * take, take)
        results.append(pltpu.make_async_copy(out_v.at[at], out.at[at], out_sem.at[g]))
        results[-1].start()
    for copy in results:
        copy.wait()


def sine_turns(y):
    z = y * y
    terms = [(-1) ** i * (2.0 * math.pi) ** (2 * i + 1) / math.factorial(2 * i + 1) for i in range(6)]
    acc = jnp.full_like(z, terms[-1])
    for term in terms[-2::-1]:
        acc = acc * z + term
    return acc * y


def turn_trig(whole, length):
    inverse = 1.0 / length
    rest = whole - jnp.round(whole * inverse) * length
    x = rest * inverse
    size = jnp.abs(x)
    sine = sine_turns(0.25 - jnp.abs(size - 0.25))
    return sine_turns(0.25 - size), jnp.where(x < 0.0, -sine, sine)


def wide_middle_kernel(waves, tiles, cols, lat_count, rows, full_rows, *refs):
    (coef, ids_in, out, wsend, fx, gsend, grecv, psend, precv, bsend, brecv, tab, hot, mix,
     weights, low_c, low_s, base_c, base_s, ids, ids_sem, s1, r1, s2, r2, s3, r3, s4, r4) = refs
    wave, tile = lax.axis_index("wave"), lax.axis_index("tile")
    slots = coef.shape[0]
    span = coef.shape[1] // waves
    packed = LANES // span
    part = slots // packed
    quarter = HALF // 4
    pairs = HALF
    chunk = full_rows // 2 // tiles
    half_rows = full_rows // 2
    block = ROWS
    blocks = rows // block

    def exchange(axis, here, count, src, dst, send, recv):
        copies = []
        for off in range(1, count):
            peer = lax.rem(here + off, count)
            copy = pltpu.make_async_remote_copy(
                src_ref=src.at[peer], dst_ref=dst.at[here], send_sem=send.at[off],
                recv_sem=recv.at[off], device_id={axis: peer}, device_id_type=MESH,
            )
            copy.start()
            copies.append(copy)
        dst[here] = src[here]
        return copies

    def finish(axis, here, count, src, dst, send, recv):
        for off in range(1, count):
            origin = lax.rem(here + count - off, count)
            pltpu.make_async_remote_copy(
                src_ref=src.at[origin], dst_ref=dst.at[origin], send_sem=send.at[off],
                recv_sem=recv.at[off], device_id={axis: origin}, device_id_type=MESH,
            ).wait_recv()

    ids_copy = pltpu.make_async_copy(ids_in, ids, ids_sem)
    ids_copy.start()
    barrier = pltpu.get_barrier_semaphore()
    for axis, here, count in (("wave", wave, waves), ("tile", tile, tiles)):
        for off in range(1, count):
            pl.semaphore_signal(
                barrier, inc=1, device_id={axis: lax.rem(here + off, count)}, device_id_type=MESH
            )

    lane = iota((1, LANES), 1)
    for w in range(waves):
        at = w * span // LANES * LANES
        place = w * span % LANES // span
        piece = None
        for j in range(packed):
            x = coef[j * part : (j + 1) * part, at : at + LANES].astype(F32)
            if j != place:
                x = pltpu.roll(x, (j - place) * span % LANES, 1)
            piece = x if piece is None else jnp.where(lane // span == j, x, piece)
        wsend[w] = piece.astype(BF16)

    polar = wave * HALF // (lat_count // 2)
    n0, n1 = 20 + 4 * polar, 20 + 4 * (HALF_LATS - 1 - polar)
    count0, count1 = n0 // 8 + 1, n1 // 8 + 1
    first = (count0 + block - 1) // block
    start1 = first * block

    j = iota((1, 2 * pairs), 1)
    upper = j >= pairs
    order = j - jnp.where(upper, pairs, 0)
    q = 4 * (order % quarter) + order // quarter
    number = jnp.where(upper, MW - 1 - q, q)
    m = number.astype(F32)
    row = iota((2 * block, 1), 0)
    low_n = jnp.where(row >= block, n1, n0).astype(F32)
    low_c[...], low_s[...] = turn_trig((row % block).astype(F32) * m, low_n)

    pl.semaphore_wait(barrier, waves + tiles - 2)
    sends = exchange("wave", wave, waves, wsend, fx, s1, r1)

    row = iota((base_c.shape[0], 1), 0)
    base_k = block * jnp.where(row >= first, row - first, row)
    base_n = jnp.where(row >= first, n1, n0).astype(F32)
    base_c[...], base_s[...] = turn_trig(base_k.astype(F32) * m, base_n)

    def fill(b, carry):
        later = (b - first + 2 * blocks) // (2 * blocks)
        low = pl.ds(pl.multiple_of(later * block, block), block)
        at = pl.ds(pl.multiple_of(b * block, block), block)
        ac, as_ = base_c[pl.ds(b, 1), :], base_s[pl.ds(b, 1), :]
        bc, bs = low_c[low, :], low_s[low, :]
        tab[at, : 2 * pairs] = (ac * bc - as_ * bs).astype(BF16)
        tab[at, 2 * pairs :] = (as_ * bc + ac * bs).astype(BF16)
        return carry

    lax.fori_loop(0, blocks, fill, 0, unroll=2)

    ids_copy.wait()
    pair = ids[...].reshape(1, ids.shape[0])
    place = iota((pairs, 1), 0)
    hot[...] = jnp.where(pair == 4 * (place % quarter) + place // quarter, 1.0, 0.0).astype(BF16)

    shape = (4 * cols, 2 * LANES)
    src, dst = iota(shape, 0), iota(shape, 1)
    same_col = src % (2 * cols) == dst % (2 * cols)
    start = src // (2 * cols) + dst // LANES * (1 + 2 * (dst // (2 * cols) % 2))
    start = jnp.where(same_col, start, 1)
    step = jnp.where(same_col, dst % LANES // (4 * cols), 0)
    for r in range(4):
        v = (start + r * step) % 4
        rule = jnp.where(v == 0, 2.0, jnp.where(v == 2, -2.0, 0.0)).astype(BF16)
        blank = jnp.zeros_like(rule)
        mix[0, r] = jnp.concatenate([rule, blank] * packed)
        mix[1, 3 - r] = jnp.concatenate([blank, rule] * packed)

    lat_lane = lane // cols % 2
    n_lane = jnp.where(lat_lane == 1, n1, n0)
    four_i = 4 * iota((quarter, 1), 0)

    point = iota((half_rows, 1), 0) + half_rows * lat_lane
    k_point = jnp.where(point >= start1, point - start1, point)
    n_point = jnp.where(point >= start1, n1, n0)
    twice = (k_point == 0) | (8 * k_point == n_point)
    used = 8 * k_point <= n_point
    used = used & jnp.logical_not(twice & (lane // (2 * cols) % 2 == 1))
    used = jnp.where(used & (point < rows), 1.0, 0.0).astype(BF16)

    src, dst = iota((LANES, LANES), 0), iota((LANES, LANES), 1)
    kind = dst // (2 * cols)
    src_turn = src // (4 * cols)
    base_turn = jnp.where(kind % 4 == 3, jnp.where(kind < 4, 1, 0), jnp.where(kind == 6, 1, 0))
    even_sign = jnp.where(src_turn % 2 == 1, -1.0, 1.0)
    diff = jnp.where(src_turn == base_turn, 1.0, jnp.where(src_turn == base_turn + 2, -1.0, 0.0))
    gain = jnp.where(kind % 4 == 0, 1.0, jnp.where(kind % 4 == 1, even_sign, diff))
    gain = jnp.where((kind >= 4) & (src // (2 * cols) % 2 == 1), -gain, gain)
    gain = jnp.where(src % cols == dst % cols, gain, 0.0)
    second_half = src // cols % 2 == 1
    folding = [jnp.where(second_half, 0.0, gain), jnp.where(second_half, gain, 0.0)]
    folding = jnp.concatenate(folding, axis=1).astype(BF16)

    levels = iota((LANES, LANES), 0), iota((LANES, LANES), 1)
    same_point = levels[0] // cols == levels[1] // cols
    above = jnp.where(same_point, 1.0, 0.0).astype(BF16)
    within = jnp.where(same_point & (levels[0] % cols >= levels[1] % cols), 1.0, 0.0).astype(BF16)

    finish("wave", wave, waves, wsend, fx, s1, r1)
    pieces = []
    for w in range(waves):
        x = fx[w]
        for p in range(packed):
            pieces.append(jnp.where(lane // span == p, x, jnp.zeros((), BF16)))
    sorted_in = dot(hot[...], jnp.concatenate(pieces)).astype(BF16)
    for h in range(2):
        for r in range(4):
            x = dot(sorted_in[r * quarter : (r + 1) * quarter], mix[h, r])
            at = h * pairs + r * quarter
            col_m = four_i + r if h == 0 else MW - 1 - r - four_i
            inside = 2 * col_m < n_lane
            for x in (x[:, :LANES], x[:, LANES:]):
                if h == 0 and r == 0:
                    x = jnp.where(col_m == 0, 0.5 * x, x)
                weights[at : at + quarter] = jnp.where(inside, x, 0.0).astype(BF16)
                at += 2 * pairs
    high = dot(tab[half_rows:], weights[...])
    high = jnp.concatenate([high, jnp.zeros((full_rows - rows, LANES), F32)])
    low = dot(tab[:half_rows], weights[...])
    row = iota((half_rows, 1), 0)
    low = jnp.where(row >= start1, pltpu.roll(low, LANES - cols, 1), low)
    high = jnp.where(row + half_rows >= start1, high, pltpu.roll(high, cols, 1))
    both = jnp.where(lat_lane == 0, low, high).astype(BF16)
    for t in range(tiles):
        gsend[t] = both[t * chunk : (t + 1) * chunk]
    sends += exchange("tile", tile, tiles, gsend, grecv, s2, r2)
    finish("tile", tile, tiles, gsend, grecv, s2, r2)

    per_f = tiles // 4
    layers = cols * per_f
    for t in range(per_f):
        u, w_ = grecv[t].astype(F32), grecv[per_f + t].astype(F32)
        t16 = grecv[2 * per_f + t]
        geo = dot(t16, within)
        for other in range(t + 1, per_f):
            geo = geo + dot(grecv[2 * per_f + other], above)
        temp, wet = t16.astype(F32), grecv[3 * per_f + t].astype(F32)
        energy = 0.5 * (u * u + w_ * w_) + geo / math.sqrt(layers)
        for f, x in enumerate((energy, u * temp, w_ * temp, u * wet)):
            psend[f * per_f + t] = x.astype(BF16)
    sends += exchange("tile", tile, tiles, psend, precv, s3, r3)

    row = iota((2 * cols, 1), 0)
    n_row = jnp.where(row >= cols, n1, n0)
    cycle = jnp.where(row >= cols, HALF_LATS - 1 - polar, polar)
    weight = 40.0 * jnp.sin(math.pi * (cycle.astype(F32) + 0.5) / (2.0 * HALF_LATS))
    weight = weight / jnp.sqrt(lat_count * n_row.astype(F32))
    weight = jnp.where(2 * number < n_row, weight, 0.0)
    residue = number % 4
    point = iota((LANES, full_rows), 1)
    lat_row = iota((LANES, full_rows), 0) // cols % 2
    own = (lat_row == 1) == (point >= start1)

    finish("tile", tile, tiles, psend, precv, s3, r3)
    back = jnp.concatenate([precv[t] for t in range(tiles)]) * used
    back = dot(back, folding)
    back = jnp.concatenate([back[:, :LANES], back[:, LANES:]]).T
    back = jnp.where(own, back, 0.0).astype(BF16)[:, :rows]
    cos_out = dot(back[: LANES // 2], tab[:, : 2 * pairs])
    sin_out = dot(back[LANES // 2 :], tab[:, 2 * pairs :])
    step = 2 * cols
    c0, c1, c2, c3 = [cos_out[i * step : (i + 1) * step] for i in range(4)]
    d0, d1, d2, d3 = [sin_out[i * step : (i + 1) * step] for i in range(4)]
    is0, is1, is2 = residue == 0, residue == 1, residue == 2
    real = jnp.where(is0, c0, jnp.where(is2, c1, c2 + jnp.where(is1, -d2, d2))) * weight
    other = jnp.where(is0, -d0, jnp.where(is2, -d1, jnp.where(is1, -c3, c3) - d3)) * weight
    rows_out = jnp.concatenate(
        [x[:, h * pairs : (h + 1) * pairs] for h in range(2) for x in (real, other)]
    ).astype(BF16)
    res = dot(rows_out, hot[...]).astype(BF16)
    for w in range(waves):
        bsend[w] = res[:, w * slots : (w + 1) * slots]
    sends += exchange("wave", wave, waves, bsend, brecv, s4, r4)
    finish("wave", wave, waves, bsend, brecv, s4, r4)
    result = jnp.concatenate([brecv[w].astype(F32) for w in range(waves)])
    out[...] = result.T
    for copy in sends:
        copy.wait_send()


def wide_middle(coef, ids, waves, tiles, cols, lat_count):
    slots, lanes = coef.shape
    span = lanes // waves
    packed = LANES // span
    rows = (NPTS // 8 + 2 + 2 * (ROWS - 1)) // ROWS * ROWS
    unit = 2 * tiles * ROWS
    full_rows = -(-rows // unit) * unit
    base_rows = -(-(rows // ROWS) // 8) * 8
    dma = pltpu.SemaphoreType.DMA
    vmem = pl.BlockSpec(memory_space=pltpu.VMEM)
    first = (waves, slots // packed, LANES)
    chunk = (tiles, full_rows // 2 // tiles, LANES)
    last = (waves, span, slots)
    return pl.pallas_call(
        functools.partial(wide_middle_kernel, waves, tiles, cols, lat_count, rows, full_rows),
        out_shape=jax.ShapeDtypeStruct((slots, lanes), F32),
        in_specs=[vmem, pl.BlockSpec(memory_space=pltpu.HBM)],
        out_specs=vmem,
        scratch_shapes=[
            pltpu.VMEM(first, BF16), pltpu.VMEM(first, BF16),
            pltpu.VMEM(chunk, BF16), pltpu.VMEM(chunk, BF16),
            pltpu.VMEM(chunk, BF16), pltpu.VMEM(chunk, BF16),
            pltpu.VMEM(last, BF16), pltpu.VMEM(last, BF16),
            pltpu.VMEM((rows, 4 * HALF), BF16),
            pltpu.VMEM((HALF, waves * slots), BF16),
            pltpu.VMEM((2, 4, LANES, 2 * LANES), BF16),
            pltpu.VMEM((4 * HALF, LANES), BF16),
            pltpu.VMEM((2 * ROWS, 2 * HALF), F32), pltpu.VMEM((2 * ROWS, 2 * HALF), F32),
            pltpu.VMEM((base_rows, 2 * HALF), F32), pltpu.VMEM((base_rows, 2 * HALF), F32),
            pltpu.VMEM(ids.shape, jnp.int32), dma,
            dma((waves,)), dma((waves,)), dma((tiles,)), dma((tiles,)),
            dma((tiles,)), dma((tiles,)), dma((waves,)), dma((waves,)),
        ],
        compiler_params=pltpu.CompilerParams(
            collective_id=0, has_side_effects=True, vmem_limit_bytes=40 * 2**20
        ),
        name="middle",
    )(coef, ids)


def wide_local(spectral, legendre, pair_ids):
    slots, _, cols, row_total = spectral.shape
    lat_count = legendre.shape[1]
    waves, tiles = lax.axis_size("wave"), lax.axis_size("tile")
    take = 4 * UNIT
    lanes = 4 * lat_count * cols
    vmem = pl.BlockSpec(memory_space=pltpu.VMEM)
    hbm = pl.BlockSpec(memory_space=pltpu.HBM)
    dma = pltpu.SemaphoreType.DMA((slots // take,))
    params = pltpu.CompilerParams(vmem_limit_bytes=52 * 2**20)
    scratch = [
        pltpu.VMEM(spectral.shape, BF16), pltpu.VMEM((slots * ROWS, UNIT * ROWS), BF16), dma, dma,
        pltpu.SMEM(pair_ids.shape, jnp.int32), pltpu.SemaphoreType.DMA,
    ]
    leg_v = pltpu.VMEM(legendre.shape, BF16)
    coef = pl.pallas_call(
        functools.partial(wide_forward_kernel, take, waves),
        out_shape=jax.ShapeDtypeStruct((slots, lanes), BF16),
        in_specs=[hbm, hbm, hbm],
        out_specs=vmem,
        scratch_shapes=[scratch[0], leg_v] + scratch[1:],
        compiler_params=params,
        name="forward",
    )(pair_ids, spectral, legendre)
    back = wide_middle(coef, pair_ids, waves, tiles, cols, lat_count)
    return pl.pallas_call(
        functools.partial(wide_inverse_kernel, take, waves),
        out_shape=jax.ShapeDtypeStruct(spectral.shape, BF16),
        in_specs=[hbm, vmem, hbm],
        out_specs=hbm,
        scratch_shapes=[leg_v] + scratch,
        compiler_params=params,
        name="inverse",
    )(pair_ids, back, legendre)


def pick(spectral, legendre, pair_ids):
    slots, _, cols, _ = spectral.shape
    fits = 2 * cols == ROWS and 2 * legendre.shape[1] == ROWS and slots % (4 * UNIT) == 0
    fits = fits and lax.axis_size("wave") * 2 == legendre.shape[1]
    return (wide_local if fits else local)(spectral, legendre, pair_ids)


def solution(mesh):
    placed = (P("wave", None, "tile", None), P("wave", None, None), P())
    return jax.shard_map(
        pick, mesh=mesh, in_specs=placed, out_specs=P("wave", None, "tile", None), check_vma=False
    )
```

```python
import functools
import math

import jax
import jax.numpy as jnp
from jax import lax
from jax.experimental import pallas as pl
from jax.experimental.pallas import tpu as pltpu
from jax.sharding import PartitionSpec as P

MW = 1280
HALF_LATS = 1280
PAIRS = 640
NPTS = 5156
LANES = 128
RADIX = 32

F32 = jnp.float32
BF16 = jnp.bfloat16

HALF = MW // 2
GROUP = HALF // 2
GPAD = -(-GROUP // LANES) * LANES
BLOCKS = GPAD // RADIX
SPAN = 16
AHEAD = 3
MESH = pl.DeviceIdType.MESH
NT = (((1,), (1,)), ((), ()))


def dot(a, b):
    return jnp.dot(a, b, preferred_element_type=F32)


def dot_nt(a, b):
    return lax.dot_general(a, b, NT, preferred_element_type=F32)


def middle_kernel(waves, tiles, cols, lat_count, kpad, *refs):
    (coef, ids, out, fx, gsend, grecv, psend, precv, bsend, trig_t, small_c, small_s, hot,
     s1, r1, s2, r2, s3, r3, s4, r4) = refs
    wave, tile = lax.axis_index("wave"), lax.axis_index("tile")
    quarter = NPTS // 4
    halves = 4 * kpad // tiles
    per_d = tiles // 4
    rows = 2 * cols
    slots = coef.shape[2]

    def exchange(axis, here, count, src, dst, send, recv):
        copies = []
        for off in range(1, count):
            peer = lax.rem(here + off, count)
            copy = pltpu.make_async_remote_copy(
                src_ref=src.at[peer], dst_ref=dst.at[here], send_sem=send.at[off],
                recv_sem=recv.at[off], device_id={axis: peer}, device_id_type=MESH,
            )
            copy.start()
            copies.append(copy)
        dst[here] = src[here]
        return copies

    def finish(axis, here, count, src, dst, send, recv):
        for off in range(1, count):
            origin = lax.rem(here + count - off, count)
            pltpu.make_async_remote_copy(
                src_ref=src.at[origin], dst_ref=dst.at[origin], send_sem=send.at[off],
                recv_sem=recv.at[off], device_id={axis: origin}, device_id_type=MESH,
            ).wait_recv()

    barrier = pltpu.get_barrier_semaphore()
    for axis, here, count in (("wave", wave, waves), ("tile", tile, tiles)):
        for off in range(1, count):
            pl.semaphore_signal(
                barrier, inc=1, device_id={axis: lax.rem(here + off, count)}, device_id_type=MESH
            )

    polar = wave * HALF // (lat_count // 2)
    q0 = 5 + polar
    n0, n1 = 4 * q0, NPTS - 4 * q0

    def line(shape, axis):
        return lax.broadcasted_iota(jnp.int32, shape, axis)

    k = line((1, kpad), 1)
    second = k >= q0
    inside = k < quarter
    point = jnp.where(inside, k - jnp.where(second, q0, 0), 0).astype(F32)
    length = jnp.where(second, n1, n0).astype(F32)

    def trig(m):
        whole = m.astype(F32) * point
        phase = whole - jnp.floor(whole / length) * length
        angle = (2.0 * math.pi) * phase / length
        return jnp.cos(angle), jnp.sin(angle)

    r = line((RADIX, 1), 0)
    m = jnp.where(r < 8, 2 * r, 16 * (r - 8))
    m = jnp.where(r >= 12, (r - 12) // 2 * HALF + (r - 12) % 2, m)
    m = jnp.where(r >= 16, 2 * RADIX * (r - 16), m)
    c, s = trig(m)
    outer = 4 * SPAN
    for g in range(4):
        ca, sa, cb, sb = c[16:], s[16:], c[12 + g : 13 + g], s[12 + g : 13 + g]
        small_c[g * SPAN : (g + 1) * SPAN] = ca * cb - sa * sb
        small_s[g * SPAN : (g + 1) * SPAN] = sa * cb + ca * sb
        ca, sa, cb, sb = c[:8], s[:8], c[8 + g : 9 + g], s[8 + g : 9 + g]
        small_c[outer + 8 * g : outer + 8 * g + 8] = ca * cb - sa * sb
        small_s[outer + 8 * g : outer + 8 * g + 8] = sa * cb + ca * sb

    pl.semaphore_wait(barrier, waves + tiles - 2)
    sends = exchange("wave", wave, waves, coef, fx, s1, r1)

    def block(idx, carry):
        g, a = idx // BLOCKS, idx % BLOCKS
        row_a = g * SPAN + a
        ac, as_ = small_c[pl.ds(row_a, 1), :], small_s[pl.ds(row_a, 1), :]
        bc, bs = small_c[outer:, :], small_s[outer:, :]
        at = ((g % 2) * 4 + g // 2) * GPAD + a * RADIX
        cos_at = pl.ds(pl.multiple_of(at, RADIX), RADIX)
        sin_at = pl.ds(pl.multiple_of(at + 2 * GPAD, RADIX), RADIX)
        trig_t[cos_at, :] = (ac * bc - as_ * bs).astype(BF16)
        trig_t[sin_at, :] = (as_ * bc + ac * bs).astype(BF16)
        return carry

    lax.fori_loop(0, 4 * BLOCKS, block, 0)

    lane = line((2 * GPAD, 1), 0)
    par = jnp.where(lane >= GPAD, 1, 0)
    i = lane - par * GPAD
    low = jnp.where(i < GROUP, 2 * i + par, -1)
    high = jnp.where(i < GROUP, HALF - 1 - par - 2 * i, -1)
    pair = ids[...].reshape(1, ids.shape[0])
    hot[0] = jnp.where(pair == low, 1.0, 0.0).astype(BF16)
    hot[1] = jnp.where(pair == high, 1.0, 0.0).astype(BF16)

    row = line((rows, 1), 0)
    n_row = jnp.where(row >= cols, n1, n0)
    cycle = jnp.where(row >= cols, HALF_LATS - 1 - polar, polar)
    weight = 40.0 * jnp.sin(math.pi * (cycle.astype(F32) + 0.5) / (2.0 * HALF_LATS))
    weight = weight / jnp.sqrt(lat_count * n_row.astype(F32))
    ii = line((1, GPAD), 1)
    up = ii % 2 == 0
    sign = jnp.where(up, 1.0, -1.0)

    def wavenumber(h, p):
        return h * HALF + p + 2 * ii

    def table(p):
        return trig_t[p * 4 * GPAD : (p + 1) * 4 * GPAD, :]

    finish("wave", wave, waves, coef, fx, s1, r1)
    terms = [[[], []], [[], []]]
    for h in range(2):
        here = [fx[w, h * 2 * rows : (h + 1) * 2 * rows, :] for w in range(waves)]
        both = dot_nt(jnp.concatenate(here, axis=1), hot[h])
        for p in range(2):
            m = wavenumber(h, p)
            factor = jnp.where(2 * m < n_row, jnp.where(m == 0, 1.0, 2.0), 0.0)
            part = both[:, p * GPAD : (p + 1) * GPAD]
            re, im = part[:rows] * factor, part[rows:] * factor
            cos_side, sin_side = ((re, re), (-im, -im)) if p == 0 else ((re, im), (-im, re))
            for x, (a, b) in enumerate((cos_side, sin_side)):
                terms[p][x].append(jnp.concatenate([a, b * sign]).astype(BF16))
    even = dot(jnp.concatenate(terms[0][0] + terms[0][1], axis=1), table(0))
    odd = dot(jnp.concatenate(terms[1][0] + terms[1][1], axis=1), table(1))

    def lat_of(x, v):
        return jnp.where(
            second, x[v * rows + cols : (v + 1) * rows], x[v * rows : v * rows + cols]
        )

    e0, e1, o0, o1 = lat_of(even, 0), lat_of(even, 1), lat_of(odd, 0), lat_of(odd, 1)
    for d, x in enumerate((e0 + o0, e1 - o1, e0 - o0, e1 + o1)):
        x = x.astype(BF16)
        for t in range(per_d):
            gsend[d * per_d + t] = x[:, t * halves : (t + 1) * halves]
    sends += exchange("tile", tile, tiles, gsend, grecv, s2, r2)
    finish("tile", tile, tiles, gsend, grecv, s2, r2)

    layers = cols * tiles // 4
    per_f = tiles // 4

    def field(f):
        return jnp.concatenate([grecv[f * per_f + t] for t in range(per_f)])

    u, w_, q = field(0).astype(F32), field(1).astype(F32), field(3).astype(F32)
    t16 = field(2)
    tri = jnp.where(line((layers, layers), 1) >= line((layers, layers), 0), 1.0, 0.0)
    geo = dot(tri.astype(BF16), t16) / math.sqrt(layers)
    temp = t16.astype(F32)
    for f, x in enumerate((0.5 * (u * u + w_ * w_) + geo, u * temp, w_ * temp, u * q)):
        x = x.astype(BF16)
        for t in range(per_f):
            psend[f * per_f + t] = x[t * cols : (t + 1) * cols]
    sends += exchange("tile", tile, tiles, psend, precv, s3, r3)
    finish("tile", tile, tiles, psend, precv, s3, r3)

    def quadrant(d):
        x = jnp.concatenate([precv[d * per_d + t].astype(F32) for t in range(per_d)], axis=1)
        return jnp.where(inside, x, 0.0)

    x0, x1, x2, x3 = [quadrant(d) for d in range(4)]

    def by_lat(*variants):
        return jnp.concatenate(
            [jnp.where(keep, v, 0.0) for v in variants for keep in (k < q0, second)]
        ).astype(BF16)

    even_in = by_lat((x0 + x2) + (x1 + x3), (x0 + x2) - (x1 + x3))
    odd_in = by_lat(x0 - x2, x1 - x3)
    even_out, odd_out = dot_nt(even_in, table(0)), dot_nt(odd_in, table(1))
    for h in range(2):
        at_c, at_s = slice(h * GPAD, (h + 1) * GPAD), slice((2 + h) * GPAD, (3 + h) * GPAD)
        ec, es, oc, os_ = even_out[:, at_c], even_out[:, at_s], odd_out[:, at_c], odd_out[:, at_s]
        keep_e = jnp.where(2 * wavenumber(h, 0) < n_row, weight, 0.0)
        keep_o = jnp.where(2 * wavenumber(h, 1) < n_row, weight, 0.0)
        e_re = jnp.where(up, ec[:rows], ec[rows:]) * keep_e
        e_im = -jnp.where(up, es[:rows], es[rows:]) * keep_e
        o_re = (oc[:rows] - sign * os_[rows:]) * keep_o
        o_im = (-os_[:rows] - sign * oc[rows:]) * keep_o
        e_both = jnp.concatenate([e_re, e_im]).astype(BF16)
        o_both = jnp.concatenate([o_re, o_im]).astype(BF16)
        res = (dot(e_both, hot[h, :GPAD]) + dot(o_both, hot[h, GPAD:])).astype(BF16)
        for w in range(waves):
            bsend[w, h * 2 * rows : (h + 1) * 2 * rows, :] = res[:, w * slots : (w + 1) * slots]
    sends += exchange("wave", wave, waves, bsend, out, s4, r4)
    finish("wave", wave, waves, bsend, out, s4, r4)
    for copy in sends:
        copy.wait_send()


def middle(coef, ids, waves, tiles, cols, lat_count):
    slots = coef.shape[2]
    step = max(tiles // 4, 1) * LANES
    kpad = -(-(NPTS // 4) // step) * step
    chunk = (tiles, cols, 4 * kpad // tiles)
    dma = pltpu.SemaphoreType.DMA
    vmem = pl.BlockSpec(memory_space=pltpu.VMEM)
    return pl.pallas_call(
        functools.partial(middle_kernel, waves, tiles, cols, lat_count, kpad),
        out_shape=jax.ShapeDtypeStruct(coef.shape, BF16),
        in_specs=[vmem, vmem],
        out_specs=vmem,
        scratch_shapes=[
            pltpu.VMEM(coef.shape, BF16),
            pltpu.VMEM(chunk, BF16), pltpu.VMEM(chunk, BF16),
            pltpu.VMEM(chunk, BF16), pltpu.VMEM(chunk, BF16),
            pltpu.VMEM(coef.shape, BF16),
            pltpu.VMEM((8 * GPAD, kpad), BF16),
            pltpu.VMEM((4 * SPAN + RADIX, kpad), F32),
            pltpu.VMEM((4 * SPAN + RADIX, kpad), F32),
            pltpu.VMEM((2, 2 * GPAD, waves * slots), BF16),
            dma((waves,)), dma((waves,)), dma((tiles,)), dma((tiles,)),
            dma((tiles,)), dma((tiles,)), dma((waves,)), dma((waves,)),
        ],
        compiler_params=pltpu.CompilerParams(
            collective_id=0, has_side_effects=True, vmem_limit_bytes=40 * 2**20
        ),
        name="middle",
    )(coef, ids)


def halves_of(ids, block, base):
    lane = lax.broadcasted_iota(jnp.int32, block.shape[1:], 1)
    parts = []
    for b in range(block.shape[0]):
        rows = block[b].astype(F32)
        low = lane < MW - ids[base + b]
        both = [jnp.where(low, rows, 0.0), jnp.where(low, 0.0, rows)]
        parts.append(jnp.concatenate(both).astype(BF16))
    return jnp.concatenate(parts)


def same_slot(shape, rows, columns):
    row = lax.broadcasted_iota(jnp.int32, shape, 0) // rows
    return row == lax.broadcasted_iota(jnp.int32, shape, 1) // columns


def fold(rows, columns):
    row = lax.broadcasted_iota(jnp.int32, (rows, columns), 0) % columns
    same = row == lax.broadcasted_iota(jnp.int32, (rows, columns), 1)
    return jnp.where(same, 1.0, 0.0).astype(BF16)


def forward_kernel(take, ids, spectral, legendre, out, spec_v, leg_v, spec_sem, leg_sem):
    slots, lats, row_total = legendre.shape
    fields = spectral.shape[1] * spectral.shape[2]
    base = lax.axis_index("wave") * slots
    copies = []
    for g in range(slots // take):
        at = pl.ds(g * take, take)
        pair = [
            pltpu.make_async_copy(legendre.at[at], leg_v.at[at], leg_sem.at[g]),
            pltpu.make_async_copy(spectral.at[at], spec_v.at[at], spec_sem.at[g]),
        ]
        copies.append(pair)
    for pair in copies[:AHEAD]:
        for copy in pair:
            copy.start()
    shape = (take * 2 * lats, take * fields)
    same = same_slot(shape, 2 * lats, fields)
    folded = fold(take * fields, fields)
    for g, pair in enumerate(copies):
        for copy in pair:
            copy.wait()
        for copy in copies[g + AHEAD] if g + AHEAD < len(copies) else ():
            copy.start()
        here = slice(g * take, (g + 1) * take)
        left = halves_of(ids, leg_v[here], base + g * take)
        right = spec_v[here].astype(F32).reshape(take * fields, row_total).astype(BF16)
        full = jnp.where(same, dot_nt(left, right), 0.0).astype(BF16)
        full = dot(full, folded).astype(BF16)
        out[here] = full.reshape((take,) + out.shape[1:])


def inverse_kernel(take, ids, back, legendre, out, leg_v, out_v, leg_sem, out_sem):
    slots, lats, row_total = legendre.shape
    fields = out.shape[1] * out.shape[2]
    base = lax.axis_index("wave") * slots
    copies = []
    for g in range(slots // take):
        at = pl.ds(g * take, take)
        copies.append(pltpu.make_async_copy(legendre.at[at], leg_v.at[at], leg_sem.at[g]))
        copies[-1].start()
    shape = (take * fields, take * 2 * lats)
    same = same_slot(shape, fields, 2 * lats)
    folded = fold(take * 2 * lats, 2 * lats)
    results = []
    for g, copy in enumerate(copies):
        at = pl.ds(g * take, take)
        here = slice(g * take, (g + 1) * take)
        narrow = back[here].reshape(take * fields, 2 * lats)
        wide = jnp.where(same, dot_nt(narrow, folded), 0.0).astype(BF16)
        copy.wait()
        right = halves_of(ids, leg_v[here], base + g * take)
        out_v[here] = dot(wide, right).reshape((take,) + out.shape[1:]).astype(BF16)
        results.append(pltpu.make_async_copy(out_v.at[at], out.at[at], out_sem.at[g]))
        results[-1].start()
    for copy in results:
        copy.wait()


def local(spectral, legendre, pair_ids):
    slots, _, cols, row_total = spectral.shape
    lat_count = legendre.shape[1]
    waves, tiles = lax.axis_size("wave"), lax.axis_size("tile")
    take = max(b for b in range(1, 17) if slots % b == 0)
    groups = slots // take
    smem = pl.BlockSpec(memory_space=pltpu.SMEM)
    vmem = pl.BlockSpec(memory_space=pltpu.VMEM)
    hbm = pl.BlockSpec(memory_space=pl.ANY)
    dma = pltpu.SemaphoreType.DMA((groups,))
    params = pltpu.CompilerParams(vmem_limit_bytes=60 * 2**20)
    coef = pl.pallas_call(
        functools.partial(forward_kernel, take),
        out_shape=jax.ShapeDtypeStruct((slots, 2 * lat_count, 2 * cols), BF16),
        in_specs=[smem, hbm, hbm],
        out_specs=vmem,
        scratch_shapes=[
            pltpu.VMEM(spectral.shape, BF16), pltpu.VMEM(legendre.shape, BF16), dma, dma,
        ],
        compiler_params=params,
        name="forward",
    )(pair_ids, spectral, legendre)
    coef = coef.reshape(slots, 2, waves, 2, 2, cols).transpose(2, 1, 4, 3, 5, 0)
    coef = coef.reshape(waves, 8 * cols, slots)
    back = middle(coef, pair_ids, waves, tiles, cols, lat_count)
    back = back.reshape(waves, 2, 2, 2, cols, slots).transpose(5, 2, 4, 1, 0, 3)
    back = back.reshape(slots, 2 * cols, 2 * lat_count)
    return pl.pallas_call(
        functools.partial(inverse_kernel, take),
        out_shape=jax.ShapeDtypeStruct(spectral.shape, BF16),
        in_specs=[smem, vmem, hbm],
        out_specs=hbm,
        scratch_shapes=[
            pltpu.VMEM(legendre.shape, BF16), pltpu.VMEM(spectral.shape, BF16), dma, dma,
        ],
        compiler_params=params,
        name="inverse",
    )(pair_ids, back, legendre)


ROWS = 16
UNIT = 8


def iota(shape, axis):
    return lax.broadcasted_iota(jnp.int32, shape, axis)


def split_rows(ids, block, base):
    count, lats, width = block.shape
    lower = iota((2 * lats, width), 0) < lats
    lane = iota((2 * lats, width), 1)
    pattern = jnp.where(lower, lane, -lane).astype(jnp.int16)
    side = iota((2 * lats, 1), 0) < lats
    parts = []
    for b in range(count):
        bound = MW - ids[base + b]
        limit = jnp.where(side, bound, 1 - bound).astype(jnp.int16)
        both = jnp.concatenate([block[b], block[b]])
        parts.append(jnp.where(pattern < limit, both, jnp.zeros((), BF16)))
    return jnp.concatenate(parts)


def lane_parts(shape, axis, waves, cols):
    lane = iota(shape, axis)
    lat = lane // cols % 2 + lane // (8 * cols) * 2
    field = lane % cols + lane // (2 * cols) % 2 * cols
    half = lane // (4 * cols) % 2
    return half * (2 * waves) + lat, field


def wide_forward_kernel(
    take, waves, ids_in, spectral, legendre, out,
    spec_v, leg_v, mid, spec_sem, leg_sem, ids, ids_sem
):
    slots, lats, width = legendre.shape
    cols = spectral.shape[2]
    fields = 2 * cols
    base = lax.axis_index("wave") * slots
    ids_copy = pltpu.make_async_copy(ids_in, ids, ids_sem)
    ids_copy.start()
    copies = []
    for g in range(slots // take):
        at = pl.ds(g * take, take)
        copies.append([
            pltpu.make_async_copy(legendre.at[at], leg_v.at[at], leg_sem.at[g]),
            pltpu.make_async_copy(spectral.at[at], spec_v.at[at], spec_sem.at[g]),
        ])
        for copy in copies[-1]:
            copy.start()
    n = UNIT * ROWS
    lanes = out.shape[1]
    same = same_slot((n, n), ROWS, ROWS)
    row_lane, field_lane = lane_parts((n, lanes), 1, waves, cols)
    spread = jnp.where(iota((n, lanes), 0) % ROWS == field_lane, 1.0, 0.0).astype(BF16)
    keep = iota((n, lanes), 0) % ROWS == row_lane
    gather = jnp.where(iota((ROWS, 2 * n), 0) == iota((ROWS, 2 * n), 1) // ROWS, 1.0, 0.0)
    gather = gather.astype(BF16)

    def finish(g):
        for at in range(g * take, (g + 1) * take, 2 * UNIT):
            parts = []
            for e in (at, at + UNIT):
                part = dot(mid[e * ROWS : e * ROWS + n], spread)
                parts.append(jnp.where(keep, part, 0.0).astype(BF16))
            out[at : at + 2 * UNIT] = dot(gather, jnp.concatenate(parts)).astype(out.dtype)

    ids_copy.wait()
    for g, pair in enumerate(copies):
        for copy in pair:
            copy.wait()
        if g:
            finish(g - 1)
        for at in range(g * take, (g + 1) * take, UNIT):
            here = slice(at, at + UNIT)
            left = split_rows(ids, leg_v[here], base + at)
            right = spec_v[here].astype(F32).reshape(UNIT * fields, width).astype(BF16)
            full = jnp.where(same, dot_nt(left, right), 0.0).astype(BF16)
            mid[at * ROWS : at * ROWS + n] = full
    finish(len(copies) - 1)


def wide_inverse_kernel(
    take, waves, ids_in, back, legendre, out,
    leg_v, out_v, mid, leg_sem, out_sem, ids, ids_sem
):
    slots, lats, width = legendre.shape
    cols = out.shape[2]
    base = lax.axis_index("wave") * slots
    ids_copy = pltpu.make_async_copy(ids_in, ids, ids_sem)
    ids_copy.start()
    copies = []
    for g in range(slots // take):
        at = pl.ds(g * take, take)
        copies.append(pltpu.make_async_copy(legendre.at[at], leg_v.at[at], leg_sem.at[g]))
        copies[-1].start()
    n = UNIT * ROWS
    lanes = back.shape[1]
    same = same_slot((n, n), ROWS, ROWS)
    row_lane, _ = lane_parts((lanes, n), 0, waves, cols)
    spread = jnp.where(iota((lanes, n), 1) % ROWS == row_lane, 1.0, 0.0).astype(BF16)
    _, field_lane = lane_parts((ROWS, lanes), 1, waves, cols)
    keep = iota((ROWS, lanes), 0) == field_lane

    def prepare(g):
        for at in range(g * take, (g + 1) * take, UNIT):
            rows = []
            for b in range(at, at + UNIT):
                row = jnp.broadcast_to(back[b : b + 1, :], (ROWS, lanes))
                rows.append(jnp.where(keep, row, 0.0).astype(BF16))
            wide = jnp.where(same, dot(jnp.concatenate(rows), spread), 0.0)
            mid[at * ROWS : at * ROWS + n] = wide.astype(BF16)

    prepare(0)
    ids_copy.wait()
    results = []
    for g, copy in enumerate(copies):
        copy.wait()
        if g + 1 < len(copies):
            prepare(g + 1)
        for at in range(g * take, (g + 1) * take, UNIT):
            here = slice(at, at + UNIT)
            right = split_rows(ids, leg_v[here], base + at)
            res = dot(mid[at * ROWS : at * ROWS + n], right)
            out_v[here] = res.reshape((UNIT,) + out.shape[1:]).astype(BF16)
        at = pl.ds(g * take, take)
        results.append(pltpu.make_async_copy(out_v.at[at], out.at[at], out_sem.at[g]))
        results[-1].start()
    for copy in results:
        copy.wait()


def sine_turns(y):
    z = y * y
    terms = [(-1) ** i * (2.0 * math.pi) ** (2 * i + 1) / math.factorial(2 * i + 1) for i in range(6)]
    acc = jnp.full_like(z, terms[-1])
    for term in terms[-2::-1]:
        acc = acc * z + term
    return acc * y


def turn_trig(whole, length):
    inverse = 1.0 / length
    rest = whole - jnp.round(whole * inverse) * length
    x = rest * inverse
    size = jnp.abs(x)
    sine = sine_turns(0.25 - jnp.abs(size - 0.25))
    return sine_turns(0.25 - size), jnp.where(x < 0.0, -sine, sine)


def wide_middle_kernel(waves, tiles, cols, lat_count, rows, full_rows, *refs):
    (coef, ids_in, out, wsend, fx, gsend, grecv, psend, precv, bsend, brecv, tab, hot, mix,
     weights, low_c, low_s, base_c, base_s, ids, ids_sem, s1, r1, s2, r2, s3, r3, s4, r4) = refs
    wave, tile = lax.axis_index("wave"), lax.axis_index("tile")
    slots = coef.shape[0]
    span = coef.shape[1] // waves
    packed = LANES // span
    part = slots // packed
    quarter = HALF // 4
    pairs = HALF
    chunk = full_rows // 2 // tiles
    half_rows = full_rows // 2
    block = ROWS
    blocks = rows // block

    def exchange(axis, here, count, src, dst, send, recv):
        copies = []
        for off in range(1, count):
            peer = lax.rem(here + off, count)
            copy = pltpu.make_async_remote_copy(
                src_ref=src.at[peer], dst_ref=dst.at[here], send_sem=send.at[off],
                recv_sem=recv.at[off], device_id={axis: peer}, device_id_type=MESH,
            )
            copy.start()
            copies.append(copy)
        dst[here] = src[here]
        return copies

    def finish(axis, here, count, src, dst, send, recv):
        for off in range(1, count):
            origin = lax.rem(here + count - off, count)
            pltpu.make_async_remote_copy(
                src_ref=src.at[origin], dst_ref=dst.at[origin], send_sem=send.at[off],
                recv_sem=recv.at[off], device_id={axis: origin}, device_id_type=MESH,
            ).wait_recv()

    ids_copy = pltpu.make_async_copy(ids_in, ids, ids_sem)
    ids_copy.start()
    barrier = pltpu.get_barrier_semaphore()
    for axis, here, count in (("wave", wave, waves), ("tile", tile, tiles)):
        for off in range(1, count):
            pl.semaphore_signal(
                barrier, inc=1, device_id={axis: lax.rem(here + off, count)}, device_id_type=MESH
            )

    lane = iota((1, LANES), 1)
    for w in range(waves):
        at = w * span // LANES * LANES
        place = w * span % LANES // span
        piece = None
        for j in range(packed):
            x = coef[j * part : (j + 1) * part, at : at + LANES].astype(F32)
            if j != place:
                x = pltpu.roll(x, (j - place) * span % LANES, 1)
            piece = x if piece is None else jnp.where(lane // span == j, x, piece)
        wsend[w] = piece.astype(BF16)

    polar = wave * HALF // (lat_count // 2)
    n0, n1 = 20 + 4 * polar, 20 + 4 * (HALF_LATS - 1 - polar)
    count0, count1 = n0 // 8 + 1, n1 // 8 + 1
    first = (count0 + block - 1) // block
    start1 = first * block

    j = iota((1, 2 * pairs), 1)
    upper = j >= pairs
    order = j - jnp.where(upper, pairs, 0)
    q = 4 * (order % quarter) + order // quarter
    number = jnp.where(upper, MW - 1 - q, q)
    m = number.astype(F32)
    row = iota((2 * block, 1), 0)
    low_n = jnp.where(row >= block, n1, n0).astype(F32)
    low_c[...], low_s[...] = turn_trig((row % block).astype(F32) * m, low_n)

    pl.semaphore_wait(barrier, waves + tiles - 2)
    sends = exchange("wave", wave, waves, wsend, fx, s1, r1)

    row = iota((base_c.shape[0], 1), 0)
    base_k = block * jnp.where(row >= first, row - first, row)
    base_n = jnp.where(row >= first, n1, n0).astype(F32)
    base_c[...], base_s[...] = turn_trig(base_k.astype(F32) * m, base_n)

    def fill(b, carry):
        later = (b - first + 2 * blocks) // (2 * blocks)
        low = pl.ds(pl.multiple_of(later * block, block), block)
        at = pl.ds(pl.multiple_of(b * block, block), block)
        ac, as_ = base_c[pl.ds(b, 1), :], base_s[pl.ds(b, 1), :]
        bc, bs = low_c[low, :], low_s[low, :]
        tab[at, : 2 * pairs] = (ac * bc - as_ * bs).astype(BF16)
        tab[at, 2 * pairs :] = (as_ * bc + ac * bs).astype(BF16)
        return carry

    lax.fori_loop(0, blocks, fill, 0, unroll=2)

    ids_copy.wait()
    pair = ids[...].reshape(1, ids.shape[0])
    place = iota((pairs, 1), 0)
    hot[...] = jnp.where(pair == 4 * (place % quarter) + place // quarter, 1.0, 0.0).astype(BF16)

    shape = (4 * cols, 2 * LANES)
    src, dst = iota(shape, 0), iota(shape, 1)
    same_col = src % (2 * cols) == dst % (2 * cols)
    start = src // (2 * cols) + dst // LANES * (1 + 2 * (dst // (2 * cols) % 2))
    start = jnp.where(same_col, start, 1)
    step = jnp.where(same_col, dst % LANES // (4 * cols), 0)
    for r in range(4):
        v = (start + r * step) % 4
        rule = jnp.where(v == 0, 2.0, jnp.where(v == 2, -2.0, 0.0)).astype(BF16)
        blank = jnp.zeros_like(rule)
        mix[0, r] = jnp.concatenate([rule, blank] * packed)
        mix[1, 3 - r] = jnp.concatenate([blank, rule] * packed)

    lat_lane = lane // cols % 2
    n_lane = jnp.where(lat_lane == 1, n1, n0)
    four_i = 4 * iota((quarter, 1), 0)

    point = iota((half_rows, 1), 0) + half_rows * lat_lane
    k_point = jnp.where(point >= start1, point - start1, point)
    n_point = jnp.where(point >= start1, n1, n0)
    twice = (k_point == 0) | (8 * k_point == n_point)
    used = 8 * k_point <= n_point
    used = used & jnp.logical_not(twice & (lane // (2 * cols) % 2 == 1))
    used = jnp.where(used & (point < rows), 1.0, 0.0).astype(BF16)

    src, dst = iota((LANES, LANES), 0), iota((LANES, LANES), 1)
    kind = dst // (2 * cols)
    src_turn = src // (4 * cols)
    base_turn = jnp.where(kind % 4 == 3, jnp.where(kind < 4, 1, 0), jnp.where(kind == 6, 1, 0))
    even_sign = jnp.where(src_turn % 2 == 1, -1.0, 1.0)
    diff = jnp.where(src_turn == base_turn, 1.0, jnp.where(src_turn == base_turn + 2, -1.0, 0.0))
    gain = jnp.where(kind % 4 == 0, 1.0, jnp.where(kind % 4 == 1, even_sign, diff))
    gain = jnp.where((kind >= 4) & (src // (2 * cols) % 2 == 1), -gain, gain)
    gain = jnp.where(src % cols == dst % cols, gain, 0.0)
    second_half = src // cols % 2 == 1
    folding = [jnp.where(second_half, 0.0, gain), jnp.where(second_half, gain, 0.0)]
    folding = jnp.concatenate(folding, axis=1).astype(BF16)

    levels = iota((LANES, LANES), 0), iota((LANES, LANES), 1)
    same_point = levels[0] // cols == levels[1] // cols
    above = jnp.where(same_point, 1.0, 0.0).astype(BF16)
    within = jnp.where(same_point & (levels[0] % cols >= levels[1] % cols), 1.0, 0.0).astype(BF16)

    finish("wave", wave, waves, wsend, fx, s1, r1)
    pieces = []
    for w in range(waves):
        x = fx[w]
        for p in range(packed):
            pieces.append(jnp.where(lane // span == p, x, jnp.zeros((), BF16)))
    sorted_in = dot(hot[...], jnp.concatenate(pieces)).astype(BF16)
    for h in range(2):
        for r in range(4):
            x = dot(sorted_in[r * quarter : (r + 1) * quarter], mix[h, r])
            at = h * pairs + r * quarter
            col_m = four_i + r if h == 0 else MW - 1 - r - four_i
            inside = 2 * col_m < n_lane
            for x in (x[:, :LANES], x[:, LANES:]):
                if h == 0 and r == 0:
                    x = jnp.where(col_m == 0, 0.5 * x, x)
                weights[at : at + quarter] = jnp.where(inside, x, 0.0).astype(BF16)
                at += 2 * pairs
    high = dot(tab[half_rows:], weights[...])
    high = jnp.concatenate([high, jnp.zeros((full_rows - rows, LANES), F32)])
    low = dot(tab[:half_rows], weights[...])
    row = iota((half_rows, 1), 0)
    low = jnp.where(row >= start1, pltpu.roll(low, LANES - cols, 1), low)
    high = jnp.where(row + half_rows >= start1, high, pltpu.roll(high, cols, 1))
    both = jnp.where(lat_lane == 0, low, high).astype(BF16)
    for t in range(tiles):
        gsend[t] = both[t * chunk : (t + 1) * chunk]
    sends += exchange("tile", tile, tiles, gsend, grecv, s2, r2)
    finish("tile", tile, tiles, gsend, grecv, s2, r2)

    per_f = tiles // 4
    layers = cols * per_f
    for t in range(per_f):
        u, w_ = grecv[t].astype(F32), grecv[per_f + t].astype(F32)
        t16 = grecv[2 * per_f + t]
        geo = dot(t16, within)
        for other in range(t + 1, per_f):
            geo = geo + dot(grecv[2 * per_f + other], above)
        temp, wet = t16.astype(F32), grecv[3 * per_f + t].astype(F32)
        energy = 0.5 * (u * u + w_ * w_) + geo / math.sqrt(layers)
        for f, x in enumerate((energy, u * temp, w_ * temp, u * wet)):
            psend[f * per_f + t] = x.astype(BF16)
    sends += exchange("tile", tile, tiles, psend, precv, s3, r3)

    row = iota((2 * cols, 1), 0)
    n_row = jnp.where(row >= cols, n1, n0)
    cycle = jnp.where(row >= cols, HALF_LATS - 1 - polar, polar)
    weight = 40.0 * jnp.sin(math.pi * (cycle.astype(F32) + 0.5) / (2.0 * HALF_LATS))
    weight = weight / jnp.sqrt(lat_count * n_row.astype(F32))
    weight = jnp.where(2 * number < n_row, weight, 0.0)
    residue = number % 4
    point = iota((LANES, full_rows), 1)
    lat_row = iota((LANES, full_rows), 0) // cols % 2
    own = (lat_row == 1) == (point >= start1)

    finish("tile", tile, tiles, psend, precv, s3, r3)
    back = jnp.concatenate([precv[t] for t in range(tiles)]) * used
    back = dot(back, folding)
    back = jnp.concatenate([back[:, :LANES], back[:, LANES:]]).T
    back = jnp.where(own, back, 0.0).astype(BF16)[:, :rows]
    cos_out = dot(back[: LANES // 2], tab[:, : 2 * pairs])
    sin_out = dot(back[LANES // 2 :], tab[:, 2 * pairs :])
    step = 2 * cols
    c0, c1, c2, c3 = [cos_out[i * step : (i + 1) * step] for i in range(4)]
    d0, d1, d2, d3 = [sin_out[i * step : (i + 1) * step] for i in range(4)]
    is0, is1, is2 = residue == 0, residue == 1, residue == 2
    real = jnp.where(is0, c0, jnp.where(is2, c1, c2 + jnp.where(is1, -d2, d2))) * weight
    other = jnp.where(is0, -d0, jnp.where(is2, -d1, jnp.where(is1, -c3, c3) - d3)) * weight
    rows_out = jnp.concatenate(
        [x[:, h * pairs : (h + 1) * pairs] for h in range(2) for x in (real, other)]
    ).astype(BF16)
    res = dot(rows_out, hot[...])
    whole = slots // LANES * LANES
    rest = slots - whole
    share = span * rest // LANES
    for w in range(waves):
        at = w * slots
        bsend[w, :span] = res[:, at : at + whole].astype(BF16)
        tail = res[:, at + whole : at + slots]
        tail = [tail[e : e + share] for e in range(0, span, share)]
        bsend[w, span:] = jnp.concatenate(tail, axis=1).astype(BF16)
    sends += exchange("wave", wave, waves, bsend, brecv, s4, r4)
    finish("wave", wave, waves, bsend, brecv, s4, r4)
    body = jnp.concatenate([brecv[w, :span].astype(F32) for w in range(waves)])
    out[:whole] = body.T
    tails = []
    for w in range(waves):
        tail = brecv[w, span:].astype(F32)
        tails += [tail[:, e : e + rest] for e in range(0, LANES, rest)]
    out[whole:] = jnp.concatenate(tails).T
    for copy in sends:
        copy.wait_send()


def wide_middle(coef, ids, waves, tiles, cols, lat_count):
    slots, lanes = coef.shape
    span = lanes // waves
    packed = LANES // span
    rows = (NPTS // 8 + 2 + 2 * (ROWS - 1)) // ROWS * ROWS
    unit = 2 * tiles * ROWS
    full_rows = -(-rows // unit) * unit
    base_rows = -(-(rows // ROWS) // 8) * 8
    dma = pltpu.SemaphoreType.DMA
    vmem = pl.BlockSpec(memory_space=pltpu.VMEM)
    first = (waves, slots // packed, LANES)
    chunk = (tiles, full_rows // 2 // tiles, LANES)
    last = (waves, span * slots // LANES, LANES)
    return pl.pallas_call(
        functools.partial(wide_middle_kernel, waves, tiles, cols, lat_count, rows, full_rows),
        out_shape=jax.ShapeDtypeStruct((slots, lanes), F32),
        in_specs=[vmem, pl.BlockSpec(memory_space=pltpu.HBM)],
        out_specs=vmem,
        scratch_shapes=[
            pltpu.VMEM(first, BF16), pltpu.VMEM(first, BF16),
            pltpu.VMEM(chunk, BF16), pltpu.VMEM(chunk, BF16),
            pltpu.VMEM(chunk, BF16), pltpu.VMEM(chunk, BF16),
            pltpu.VMEM(last, BF16), pltpu.VMEM(last, BF16),
            pltpu.VMEM((rows, 4 * HALF), BF16),
            pltpu.VMEM((HALF, waves * slots), BF16),
            pltpu.VMEM((2, 4, LANES, 2 * LANES), BF16),
            pltpu.VMEM((4 * HALF, LANES), BF16),
            pltpu.VMEM((2 * ROWS, 2 * HALF), F32), pltpu.VMEM((2 * ROWS, 2 * HALF), F32),
            pltpu.VMEM((base_rows, 2 * HALF), F32), pltpu.VMEM((base_rows, 2 * HALF), F32),
            pltpu.VMEM(ids.shape, jnp.int32), dma,
            dma((waves,)), dma((waves,)), dma((tiles,)), dma((tiles,)),
            dma((tiles,)), dma((tiles,)), dma((waves,)), dma((waves,)),
        ],
        compiler_params=pltpu.CompilerParams(
            collective_id=0, has_side_effects=True, vmem_limit_bytes=40 * 2**20
        ),
        name="middle",
    )(coef, ids)


def wide_local(spectral, legendre, pair_ids):
    slots, _, cols, row_total = spectral.shape
    lat_count = legendre.shape[1]
    waves, tiles = lax.axis_size("wave"), lax.axis_size("tile")
    take = 4 * UNIT
    lanes = 4 * lat_count * cols
    vmem = pl.BlockSpec(memory_space=pltpu.VMEM)
    hbm = pl.BlockSpec(memory_space=pltpu.HBM)
    dma = pltpu.SemaphoreType.DMA((slots // take,))
    params = pltpu.CompilerParams(vmem_limit_bytes=52 * 2**20)
    scratch = [
        pltpu.VMEM(spectral.shape, BF16), pltpu.VMEM((slots * ROWS, UNIT * ROWS), BF16), dma, dma,
        pltpu.SMEM(pair_ids.shape, jnp.int32), pltpu.SemaphoreType.DMA,
    ]
    leg_v = pltpu.VMEM(legendre.shape, BF16)
    coef = pl.pallas_call(
        functools.partial(wide_forward_kernel, take, waves),
        out_shape=jax.ShapeDtypeStruct((slots, lanes), BF16),
        in_specs=[hbm, hbm, hbm],
        out_specs=vmem,
        scratch_shapes=[scratch[0], leg_v] + scratch[1:],
        compiler_params=params,
        name="forward",
    )(pair_ids, spectral, legendre)
    back = wide_middle(coef, pair_ids, waves, tiles, cols, lat_count)
    return pl.pallas_call(
        functools.partial(wide_inverse_kernel, take, waves),
        out_shape=jax.ShapeDtypeStruct(spectral.shape, BF16),
        in_specs=[hbm, vmem, hbm],
        out_specs=hbm,
        scratch_shapes=[leg_v] + scratch,
        compiler_params=params,
        name="inverse",
    )(pair_ids, back, legendre)


def pick(spectral, legendre, pair_ids):
    slots, _, cols, _ = spectral.shape
    fits = 2 * cols == ROWS and 2 * legendre.shape[1] == ROWS and slots % (4 * UNIT) == 0
    fits = fits and lax.axis_size("wave") * 2 == legendre.shape[1]
    fits = fits and slots // LANES == 1 and LANES % max(slots % LANES, 1) == 0
    fits = fits and slots % LANES >= 32
    return (wide_local if fits else local)(spectral, legendre, pair_ids)


def solution(mesh):
    placed = (P("wave", None, "tile", None), P("wave", None, None), P())
    return jax.shard_map(
        pick, mesh=mesh, in_specs=placed, out_specs=P("wave", None, "tile", None), check_vma=False
    )
```
